256 devices in a mesh: image: 16 (over x_lo, z), domain: 16 (over y, x_hi, core).
Axes of the slice: x: 4 (x_hi: 2, x_lo: 2; x = x_hi * 2 + x_lo), y: 4, z: 8, core: 2. Of those that a mesh axis runs over, the one named last changes fastest.
Arguments:
- field: float32 [16, 64, 64, 128], P('image', 'domain'), may hold values from -0.9 to 1.1
- mobility: float32 [64, 64, 128], P('domain'), may hold values from 0.2 to 1
- lower: int32 [2, 16], P(None, 'image'), may hold values from 0 to 14, as said below
- weights: float32 [2, 16], P(None, 'image'), may hold values from 0 to 1
Outputs:
- evolved: float32 [16, 64, 64, 128], P('image', 'domain')
- arclength: float32 [2, 16], P(None, 'image')
The draws below stay inside these ranges and needn't reach their ends.
Inputs may be any that keep to these rules, and one draw needn't show every extreme that they name: lower[c, i] is i - 1 or i.
All inputs are finite; a program needn't handle non-finite values.
Results may differ from the reference program's by a relative error of at most 0.0001.
Values sent between devices are 32-bit elements; how exact they have to be, the bound alone decides.
No kernel may reach another device: no remote copies, remote signals or barrier semaphores. Data moves between devices by JAX's collectives and lax.ppermute only.
A program may use at most 64 MiB of HBM per device.

```python
import math
import jax
import jax.numpy as jnp
from jax import lax

NY = 64
NZ = 128
STEPS = 8
CYCLES = 2
IMAGES = 16
NX = 64


def draw_field(key, part):
    ramp_level = jnp.arange(NX, dtype=jnp.float32) / (NX - 1)
    random_part = jax.random.uniform(key, (IMAGES, NX, NY, NZ), jnp.float32, -1.0, 1.0)
    amplitude = 0.3 + 0.6 * ramp_level
    return amplitude[None, :, None, None] * random_part


def draw_lower(key, part):
    offsets = jax.random.randint(jax.random.fold_in(key, 7), (CYCLES, IMAGES), 0, 2)
    image_number = jnp.arange(IMAGES, dtype=jnp.int32)[None, :]
    return jnp.clip(image_number - 1 + offsets, 0, IMAGES - 2).astype(jnp.int32)


def steps_of(own_key, shape, split, least, largest):
    def one(dim, shards_of):
        draws = jax.random.uniform(jax.random.fold_in(jax.random.fold_in(own_key, 6), dim), (shards_of,), jnp.float32, least / len(split), largest / len(split))
        return jnp.repeat(jnp.exp(draws), shape[dim] // shards_of).reshape((-1,) + (1,) * (len(shape) - dim - 1))

    loudness = one(*split[0])
    for cut in split[1:]:
        loudness = loudness * one(*cut)
    return loudness


def setup_inputs(seed: int = 0) -> dict:
    key_of = jax.random.split(jax.random.key(seed), 5)
    field = draw_field(jax.random.fold_in(key_of[4], 71), 0)
    mobility = jnp.clip(jnp.exp(math.log(1.0) - 1.609438 * jax.random.uniform(key_of[1], (NX, NY, NZ), jnp.float32) ** steps_of(key_of[1], (NX, NY, NZ), ((0, 16),), -0.2, 0.2)), 0.2, 1.0)
    lower = draw_lower(jax.random.fold_in(key_of[4], 71), 0)
    weights = jnp.clip(1.0 * jax.random.uniform(key_of[3], (CYCLES, IMAGES), jnp.float32) ** steps_of(key_of[3], (CYCLES, IMAGES), ((1, 16),), -0.2, 0.2), 0.0, 1.0)
    return dict(field=field, mobility=mobility, lower=lower, weights=weights)


stiffness = 1.0
time_step = 0.008
epsilon = 1e-06

def advance(padded, mobile_padded):
    interior = padded[1:-1]
    laplacian = padded[2:] + padded[:-2] + jnp.roll(interior, 1, 1) + jnp.roll(interior, -1, 1) + jnp.roll(interior, 1, 2) + jnp.roll(interior, -1, 2) - 6.0 * interior
    potential = interior * interior * interior - interior - stiffness * laplacian
    motion = mobile_padded[1:-1] / (1.0 + interior * interior)
    centre = motion[1:-1]
    middle = potential[1:-1]
    change = 0.5 * (centre + motion[2:]) * (potential[2:] - middle) + 0.5 * (centre + motion[:-2]) * (potential[:-2] - middle)
    for dimension in (1, 2):
        for offset in (1, -1):
            change = change + 0.5 * (centre + jnp.roll(centre, offset, dimension)) * (jnp.roll(middle, offset, dimension) - middle)
    return padded[2:-2] + time_step * change

def wrap_rows(array, margin):
    return jnp.concatenate([array[-margin:], array, array[:margin]], axis=0)

def evolve_image(image_field, mobility):
    mobile_padded = wrap_rows(mobility, 2)
    for repeat in range(STEPS):
        image_field = advance(wrap_rows(image_field, 2), mobile_padded)
    return image_field

def reference(field, mobility, lower, weights):
    images = field
    total_cells = NX * NY * NZ
    lengths = []
    for cycle_index in range(CYCLES):
        images = lax.map(lambda single_image: evolve_image(single_image, mobility), images)
        gaps = lax.optimization_barrier(jnp.sum(jnp.square(images[1:] - images[:-1]), axis=(1, 2, 3)))
        distance = jnp.sqrt(gaps / total_cells + epsilon)
        arclength = jnp.concatenate([jnp.zeros((1,), jnp.float32), jnp.cumsum(distance)])
        lengths.append(arclength)
        first_image = jnp.take(images, lower[cycle_index], axis=0)
        second_image = jnp.take(images, lower[cycle_index] + 1, axis=0)
        weight_now = weights[cycle_index][:, None, None, None]
        images = weight_now * first_image + (1.0 - weight_now) * second_image
    return (images, jnp.stack(lengths))
```

```python
import jax
import jax.numpy as jnp
from jax import lax
from jax.experimental import pallas as pl
from jax.experimental.pallas import tpu as pltpu
from jax.sharding import PartitionSpec as P

STEPS = 8
CYCLES = 2

stiffness = 1.0
time_step = 0.008
epsilon = 1e-06

VMEM = pl.BlockSpec(memory_space=pltpu.VMEM)
SMEM = pl.BlockSpec(memory_space=pltpu.SMEM)


def fetched(value, offset):
    size = lax.axis_size("domain")
    return lax.ppermute(value, "domain", [((i + offset) % size, i) for i in range(size)])


def partnered(value):
    size = lax.axis_size("domain")
    return lax.ppermute(value, "domain", [(i ^ 1, i) for i in range(size)])


def passed_along(value, steps):
    count = lax.axis_size("image")
    first, last = (max(0, -steps), min(count, count - steps))
    return lax.ppermute(value, "image", [(i, i + steps) for i in range(first, last)])


def halo_pieces(own, parity):
    after2, before2 = fetched(own, 2), fetched(own, -2)
    after4, before4 = fetched(own, 4), fetched(own, -4)
    chosen = jnp.where(parity == 0, after4, before4)
    return (own, before4, before2, after2, after4) + tuple(
        partnered(piece) for piece in (chosen, before2, own, after2)
    )


def fill(window, parity, pieces, rows):
    own, before4, before2, after2, after4, *others = pieces
    for place, piece in ((0, before4), (2, before2), (4, own), (6, after2), (8, after4)):
        window[pl.ds(place * rows, rows)] = piece[...]

    @pl.when(parity == 0)
    def _():
        for place, piece in zip((1, 3, 5, 7), others):
            window[pl.ds(place * rows, rows)] = piece[...]

    @pl.when(parity != 0)
    def _():
        for place, piece in zip((7, 1, 3, 5), others):
            window[pl.ds(place * rows, rows)] = piece[...]


def shifted(plane, offset, dimension):
    return pltpu.roll(plane, offset % plane.shape[dimension], dimension)


def potential_and_motion(field, mobile, row):
    here = field[row]
    square = here * here
    around = field[row - 1] + field[row + 1]
    for dimension in (0, 1):
        around = around + (shifted(here, 1, dimension) + shifted(here, -1, dimension))
    potential = here * (square + 5.0) - around
    motion = mobile[row] / (1.0 + square)
    return potential, motion


def take_steps(field, mobile, length):
    for step in range(STEPS):
        first, last = 2 * step + 2, length - 2 * step - 2
        before = potential_and_motion(field, mobile, first - 1)
        now = potential_and_motion(field, mobile, first)
        inflow = (before[1] + now[1]) * (now[0] - before[0])

        def one_row(row, carried):
            potential, motion, inflow = carried
            ahead = potential_and_motion(field, mobile, row + 1)
            outflow = (motion + ahead[1]) * (ahead[0] - potential)
            change = outflow - inflow
            for dimension in (0, 1):
                flow = (motion + shifted(motion, 1, dimension)) * (
                    potential - shifted(potential, 1, dimension)
                )
                change = change + (shifted(flow, -1, dimension) - flow)
            field[row] = field[row] + change
            return ahead[0], ahead[1], outflow

        lax.fori_loop(first, last, one_row, (now[0], now[1], inflow))


def first_kernel(parity_ref, *refs):
    fields, mobiles = refs[:9], refs[9:18]
    out, mobile_out, window = refs[18:]
    rows = out.shape[0]
    parity = parity_ref[0]
    fill(window, parity, fields, rows)
    fill(mobile_out, parity, mobiles, rows)
    mobile_out[...] = mobile_out[...] * (0.5 * time_step)
    take_steps(window, mobile_out, 9 * rows)
    out[...] = window[pl.ds(4 * rows, rows)]


def later_kernel(parity_ref, *refs):
    fields, mobile, out, window = refs[:9], refs[9], refs[10], refs[11]
    rows = out.shape[0]
    fill(window, parity_ref[0], fields, rows)
    take_steps(window, mobile, 9 * rows)
    out[...] = window[pl.ds(4 * rows, rows)]


def mix_kernel(scalar_ref, weight_ref, own, left, right, out, total):
    weight = weight_ref[0]
    here, after = own[...], right[...]
    total[...] = jnp.zeros_like(total) + jnp.sum(jnp.square(after - here))

    @pl.when(scalar_ref[0] == 0)
    def _():
        out[...] = weight * left[...] + (1.0 - weight) * here

    @pl.when(scalar_ref[0] != 0)
    def _():
        out[...] = weight * here + (1.0 - weight) * after


def length_kernel(cells, images, index_ref, gaps, out):
    distance = jnp.sqrt(
        jnp.sum(gaps[...].reshape(images, -1, CYCLES, 128), axis=1) / cells + epsilon
    )
    position = lax.broadcasted_iota(jnp.int32, distance.shape, 0)
    kept = jnp.where(position < index_ref[0], distance, 0.0)
    out[...] = jnp.sum(kept, axis=0)[:, :1]


def per_device(field, mobility, lower, weights):
    shape = field.shape[1:]
    rows = shape[0]
    image_count, domain_count = lax.axis_size("image"), lax.axis_size("domain")
    image_index = lax.axis_index("image")
    parity = lax.rem(lax.axis_index("domain"), 2)
    parities = parity[None]
    cells = rows * domain_count * shape[1] * shape[2]
    plane = jax.ShapeDtypeStruct(shape, jnp.float32)
    wide = (9 * rows,) + shape[1:]
    window = pltpu.VMEM(wide, jnp.float32)

    both = halo_pieces(jnp.stack([field[0], mobility]), parity)
    phase, mobile = pl.pallas_call(
        first_kernel,
        out_shape=(plane, jax.ShapeDtypeStruct(wide, jnp.float32)),
        in_specs=[SMEM] + [VMEM] * 18,
        out_specs=(VMEM, VMEM),
        scratch_shapes=[window],
    )(parities, *(piece[0] for piece in both), *(piece[1] for piece in both))

    totals = []
    for cycle in range(CYCLES):
        if cycle:
            phase = pl.pallas_call(
                later_kernel,
                out_shape=plane,
                in_specs=[SMEM] + [VMEM] * 10,
                out_specs=VMEM,
                scratch_shapes=[window],
            )(parities, *halo_pieces(phase, parity), mobile)
        left, right = passed_along(phase, 1), passed_along(phase, -1)
        from_left = (lower[cycle] >= image_index).astype(jnp.int32)
        phase, total = pl.pallas_call(
            mix_kernel,
            out_shape=(plane, jax.ShapeDtypeStruct((1, 128), jnp.float32)),
            in_specs=[SMEM, SMEM] + [VMEM] * 3,
            out_specs=(VMEM, VMEM),
        )(from_left, weights[cycle], phase, left, right)
        totals.append(total)
    mine = jnp.concatenate(totals, axis=0)
    everyone = jnp.broadcast_to(mine[None], (image_count * domain_count, CYCLES, 128))
    gaps = lax.all_to_all(everyone, ("image", "domain"), 0, 0)
    arclength = pl.pallas_call(
        lambda *refs: length_kernel(cells, image_count, *refs),
        out_shape=jax.ShapeDtypeStruct((CYCLES, 1), jnp.float32),
        in_specs=[SMEM, VMEM],
        out_specs=VMEM,
    )(image_index[None], gaps)
    return phase[None], arclength


def solution(mesh):
    return jax.shard_map(
        per_device,
        mesh=mesh,
        in_specs=(
            P("image", "domain", None, None),
            P("domain", None, None),
            P(None, "image"),
            P(None, "image"),
        ),
        out_specs=(P("image", "domain", None, None), P(None, "image")),
        check_vma=False,
    )
```

```python
import jax
import jax.numpy as jnp
from jax import lax
from jax.experimental import pallas as pl
from jax.experimental.pallas import tpu as pltpu
from jax.sharding import PartitionSpec as P

STEPS = 8
CYCLES = 2
SUBLANES = 8
UNROLL = 4

stiffness = 1.0
time_step = 0.008
epsilon = 1e-06

VMEM = pl.BlockSpec(memory_space=pltpu.VMEM)
SMEM = pl.BlockSpec(memory_space=pltpu.SMEM)
PARAMS = pltpu.CompilerParams(vmem_limit_bytes=16 << 20)


def fetched(value, offset):
    size = lax.axis_size("domain")
    return lax.ppermute(value, "domain", [((i + offset) % size, i) for i in range(size)])


def partnered(value):
    size = lax.axis_size("domain")
    return lax.ppermute(value, "domain", [(i ^ 1, i) for i in range(size)])


def passed_along(value, steps):
    count = lax.axis_size("image")
    first, last = (max(0, -steps), min(count, count - steps))
    return lax.ppermute(value, "image", [(i, i + steps) for i in range(first, last)])


def halo_pieces(own, parity):
    after2, before2 = fetched(own, 2), fetched(own, -2)
    after4, before4 = fetched(own, 4), fetched(own, -4)
    chosen = jnp.where(parity == 0, after4, before4)
    return [own, before4, before2, after2, after4] + [
        partnered(piece) for piece in (chosen, before2, own, after2)
    ]


def fill(window, parity, pieces, rows):
    own, before4, before2, after2, after4, *others = pieces
    for place, piece in ((0, before4), (2, before2), (4, own), (6, after2), (8, after4)):
        window[pl.ds(place * rows, rows)] = piece[...]

    @pl.when(parity == 0)
    def _():
        for place, piece in zip((1, 3, 5, 7), others):
            window[pl.ds(place * rows, rows)] = piece[...]

    @pl.when(parity != 0)
    def _():
        for place, piece in zip((7, 1, 3, 5), others):
            window[pl.ds(place * rows, rows)] = piece[...]


def folded(source, row, target, place):
    folds = target.shape[-3]
    for v in range(folds):
        target[(*place, v)] = source[row, pl.ds(v, SUBLANES, stride=folds), :]


def y_shifted(value, offset):
    if offset == 1:
        return jnp.concatenate([pltpu.roll(value[-1:], 1, 1), value[:-1]], axis=0)
    return jnp.concatenate([value[1:], pltpu.roll(value[:1], SUBLANES - 1, 1)], axis=0)


def z_shifted(value, offset):
    return pltpu.roll(value, offset % value.shape[2], 2)


def potential_and_motion(field, mobile, row):
    here = field[row]
    square = here * here
    around = field[row - 1] + field[row + 1]
    for shifted in (y_shifted, z_shifted):
        around = around + (shifted(here, 1) + shifted(here, -1))
    potential = here * (square + 5.0) - around
    motion = mobile[row] / (1.0 + square)
    return potential, motion


def take_steps(field, mobile, length):
    for step in range(STEPS):
        first, last = 2 * step + 2, length - 2 * step - 2
        before = potential_and_motion(field, mobile, first - 1)
        now = potential_and_motion(field, mobile, first)
        inflow = (before[1] + now[1]) * (now[0] - before[0])

        def one_row(row, carried):
            potential, motion, inflow = carried
            ahead = potential_and_motion(field, mobile, row + 1)
            outflow = (motion + ahead[1]) * (ahead[0] - potential)
            change = outflow - inflow
            for shifted in (y_shifted, z_shifted):
                flow = (motion + shifted(motion, 1)) * (potential - shifted(potential, 1))
                change = change + (shifted(flow, -1) - flow)
            field[row] = field[row] + change
            return ahead[0], ahead[1], outflow

        lax.fori_loop(first, last, one_row, (now[0], now[1], inflow), unroll=UNROLL)


def pack_kernel(field, mobility, out):
    for row in range(field.shape[0]):
        folded(field, row, out, (0, row))
        folded(mobility, row, out, (1, row))
    out[1] = out[1] * (0.5 * time_step)


def first_kernel(parity_ref, *refs):
    pieces, out, mobile, window = refs[:9], *refs[9:]
    rows = out.shape[0]
    fill(window, parity_ref[0], [piece.at[0] for piece in pieces], rows)
    fill(mobile, parity_ref[0], [piece.at[1] for piece in pieces], rows)
    take_steps(window, mobile, 9 * rows)
    out[...] = window[pl.ds(4 * rows, rows)]


def later_kernel(parity_ref, *refs):
    pieces, mobile, out, window = refs[:9], *refs[9:]
    rows = out.shape[0]
    fill(window, parity_ref[0], pieces, rows)
    take_steps(window, mobile, 9 * rows)
    out[...] = window[pl.ds(4 * rows, rows)]


def mix_kernel(cycle, index_ref, lower_ref, weight_ref, own, left, right, *refs):
    earlier, (out, total) = refs[:-2], refs[-2:]
    weight = weight_ref[cycle, 0]
    from_left = lower_ref[cycle, 0] < index_ref[0]
    squares = jnp.square(right[...] - own[...])
    total[cycle : cycle + 1] = jnp.sum(squares, axis=(0, 1, 2))[None]
    for there in earlier:
        total[:cycle] = there[:cycle]

    def write(first, second):
        for row in range(own.shape[0]):
            mixed = weight * first[row] + (1.0 - weight) * second[row]
            if out.shape == own.shape:
                out[row] = mixed
            else:
                folds = mixed.shape[0]
                for v in range(folds):
                    out[row, pl.ds(v, SUBLANES, stride=folds), :] = mixed[v]

    @pl.when(from_left)
    def _():
        write(left, own)

    @pl.when(jnp.logical_not(from_left))
    def _():
        write(own, right)


def length_kernel(cells, images, index_ref, gaps, out):
    each = jnp.sum(gaps[...].reshape(images, -1, CYCLES, 128), axis=1)
    distance = jnp.sqrt(jnp.sum(each, axis=-1, keepdims=True) / cells + epsilon)
    position = lax.broadcasted_iota(jnp.int32, distance.shape, 0)
    kept = jnp.where(position < index_ref[0], distance, 0.0)
    out[...] = jnp.sum(kept, axis=0)


def shaped(*shape):
    return jax.ShapeDtypeStruct(shape, jnp.float32)


def per_device(field, mobility, lower, weights):
    rows, depth, lanes = field.shape[1:]
    slab = (rows, depth // SUBLANES, SUBLANES, lanes)
    wide = (9 * rows,) + slab[1:]
    window = pltpu.VMEM(wide, jnp.float32)
    image_count, domain_count = lax.axis_size("image"), lax.axis_size("domain")
    image_index = lax.axis_index("image")[None]
    parity = lax.rem(lax.axis_index("domain"), 2)
    parities = parity[None]
    cells = rows * domain_count * depth * lanes

    packed = pl.pallas_call(
        pack_kernel,
        out_shape=shaped(2, *slab),
        in_specs=[VMEM] * 2,
        out_specs=VMEM,
        compiler_params=PARAMS,
    )(field[0], mobility)
    phase, mobile = pl.pallas_call(
        first_kernel,
        out_shape=(shaped(*slab), shaped(*wide)),
        in_specs=[SMEM] + [VMEM] * 9,
        out_specs=(VMEM, VMEM),
        scratch_shapes=[window],
        compiler_params=PARAMS,
    )(parities, *halo_pieces(packed, parity))

    totals = []
    for cycle in range(CYCLES):
        if cycle:
            phase = pl.pallas_call(
                later_kernel,
                out_shape=shaped(*slab),
                in_specs=[SMEM] + [VMEM] * 10,
                out_specs=VMEM,
                scratch_shapes=[window],
                compiler_params=PARAMS,
            )(parities, *halo_pieces(phase, parity), mobile)
        left, right = passed_along(phase, 1), passed_along(phase, -1)
        after = slab if cycle < CYCLES - 1 else (rows, depth, lanes)
        phase, total = pl.pallas_call(
            lambda *refs, cycle=cycle: mix_kernel(cycle, *refs),
            out_shape=(shaped(*after), shaped(CYCLES, lanes)),
            in_specs=[SMEM] * 3 + [VMEM] * (3 + len(totals)),
            out_specs=(VMEM, VMEM),
            compiler_params=PARAMS,
        )(image_index, lower, weights, phase, left, right, *totals)
        totals = [total]
    everyone = jnp.broadcast_to(totals[0][None], (image_count * domain_count, CYCLES, lanes))
    gaps = lax.all_to_all(everyone, ("image", "domain"), 0, 0)
    arclength = pl.pallas_call(
        lambda *refs: length_kernel(cells, image_count, *refs),
        out_shape=shaped(CYCLES, 1),
        in_specs=[SMEM, VMEM],
        out_specs=VMEM,
        compiler_params=PARAMS,
    )(image_index, gaps)
    return phase[None], arclength


def solution(mesh):
    return jax.shard_map(
        per_device,
        mesh=mesh,
        in_specs=(
            P("image", "domain", None, None),
            P("domain", None, None),
            P(None, "image"),
            P(None, "image"),
        ),
        out_specs=(P("image", "domain", None, None), P(None, "image")),
        check_vma=False,
    )
```

```python
import jax
import jax.numpy as jnp
from jax import lax
from jax.experimental import pallas as pl
from jax.experimental.pallas import tpu as pltpu
from jax.sharding import PartitionSpec as P

STEPS = 8
CYCLES = 2
SUBLANES = 8
UNROLL = 4

stiffness = 1.0
time_step = 0.008
epsilon = 1e-06

VMEM = pl.BlockSpec(memory_space=pltpu.VMEM)
SMEM = pl.BlockSpec(memory_space=pltpu.SMEM)
PARAMS = pltpu.CompilerParams(vmem_limit_bytes=16 << 20)


def exchanged(value, axis, partner):
    size = lax.axis_size(axis)
    pairs = [(i, partner(i, size)) for i in range(size)]
    return lax.ppermute(value, axis, [(i, j) for i, j in pairs if 0 <= j < size])


def passed_along(value, steps):
    count = lax.axis_size("image")
    first, last = (max(0, -steps), min(count, count - steps))
    return lax.ppermute(value, "image", [(i, i + steps) for i in range(first, last)])


def side(index, stride):
    return 1 - 2 * (index // stride % 2)


def partner_inside(stride):
    return lambda i, size: i + side(i, stride) * stride


def partner_across(stride):
    return lambda i, size: (i - side(i, stride) * stride) % size


def halo_pieces(own, index):
    twos = [exchanged(own, "domain", partner(2)) for partner in (partner_across, partner_inside)]
    fours = [exchanged(own, "domain", partner(4)) for partner in (partner_across, partner_inside)]
    chosen = jnp.where(side(index, 4) == side(index, 1), fours[1], fours[0])
    return [own, *twos, *fours] + [
        exchanged(piece, "domain", partner_inside(1)) for piece in (own, *twos, chosen)
    ]


def slab_offsets(index):
    core, two, four = (side(index, stride) for stride in (1, 2, 4))
    straight = (0, -2 * two, 2 * two, -4 * four, 4 * four)
    return straight + (core, core - 2 * two, core + 2 * two, -3 * core)


def fill(window, index, pieces, rows):
    for offset, piece in zip(slab_offsets(index), pieces):
        start = pl.multiple_of((4 + offset) * rows, rows)
        window[pl.ds(start, rows)] = piece[...]


def fold(plane, target, place, scale=None):
    folds = target.shape[-3]
    for v in range(folds):
        part = plane[pl.ds(v, SUBLANES, stride=folds), :]
        target[(*place, v)] = part if scale is None else part * scale


def unfold(value, target):
    for v in range(value.shape[0]):
        target[pl.ds(v, SUBLANES, stride=value.shape[0]), :] = value[v]


def y_shifted(value, offset):
    if offset == 1:
        return jnp.concatenate([pltpu.roll(value[-1:], 1, 1), value[:-1]], axis=0)
    return jnp.concatenate([value[1:], pltpu.roll(value[:1], SUBLANES - 1, 1)], axis=0)


def z_shifted(value, offset):
    return pltpu.roll(value, offset % value.shape[2], 2)


def potential_and_motion(field, mobile, row):
    here = field[row]
    square = here * here
    around = field[row - 1] + field[row + 1]
    for shifted in (y_shifted, z_shifted):
        around = around + (shifted(here, 1) + shifted(here, -1))
    potential = here * (square + 5.0) - around
    motion = mobile[row] / (1.0 + square)
    return potential, motion


def take_steps(field, mobile, length):
    for step in range(STEPS):
        first, last = 2 * step + 2, length - 2 * step - 2
        before = potential_and_motion(field, mobile, first - 1)
        now = potential_and_motion(field, mobile, first)
        inflow = (before[1] + now[1]) * (now[0] - before[0])

        def one_row(row, carried):
            potential, motion, inflow = carried
            ahead = potential_and_motion(field, mobile, row + 1)
            outflow = (motion + ahead[1]) * (ahead[0] - potential)
            change = outflow - inflow
            for shifted in (y_shifted, z_shifted):
                flow = (motion + shifted(motion, 1)) * (potential - shifted(potential, 1))
                change = change + (shifted(flow, -1) - flow)
            field[row] = field[row] + change
            return ahead[0], ahead[1], outflow

        lax.fori_loop(first, last, one_row, (now[0], now[1], inflow), unroll=UNROLL)


def pack_kernel(field, mobility, out, held, semaphores):
    copies = [
        pltpu.make_async_copy(source, held.at[i], semaphores.at[i])
        for i, source in enumerate((field, mobility))
    ]
    for copy in copies:
        copy.start()
    for i, copy in enumerate(copies):
        copy.wait()
        for row in range(field.shape[0]):
            fold(held.at[i, row], out, (i, row), 0.5 * time_step if i else None)


def first_kernel(index_ref, *refs):
    pieces, out, mobile, window = refs[:9], *refs[9:]
    rows = out.shape[0]
    fill(window, index_ref[0], [piece.at[0] for piece in pieces], rows)
    fill(mobile, index_ref[0], [piece.at[1] for piece in pieces], rows)
    take_steps(window, mobile, 9 * rows)
    out[...] = window[pl.ds(4 * rows, rows)]


def later_kernel(index_ref, *refs):
    pieces, mobile, out, window = refs[:9], *refs[9:]
    rows = out.shape[0]
    fill(window, index_ref[0], pieces, rows)
    take_steps(window, mobile, 9 * rows)
    out[...] = window[pl.ds(4 * rows, rows)]


def squares_of(own, after):
    return jnp.sum(jnp.square(after[...] - own[...]), axis=(0, 1, 2))[None]


def mixing(cycle, image, lower_ref, weight_ref):
    from_left = lower_ref[0, cycle] < image
    weight = weight_ref[0, cycle]
    rest = 1.0 - weight
    return from_left, jnp.where(from_left, weight, rest), jnp.where(from_left, rest, weight)


def mix_kernel(cycle, index_ref, lower_ref, weight_ref, own, inside, across, out, total):
    image = index_ref[0]
    even = lax.rem(image, 2) == 0
    from_left, of_other, of_own = mixing(cycle, image, lower_ref, weight_ref)

    def when(condition, do, *refs):
        pl.when(condition)(lambda: do(*refs))

    def measure(after):
        total[...] = squares_of(own, after)

    def write(other):
        for row in range(own.shape[0]):
            out[row] = of_other * other[row] + of_own * own[row]

    when(even, measure, inside)
    when(jnp.logical_not(even), measure, across)
    when(from_left != even, write, inside)
    when(from_left == even, write, across)


def gap_kernel(own, right, earlier, total):
    total[: CYCLES - 1] = earlier[...]
    total[CYCLES - 1 :] = squares_of(own, right)


def last_kernel(cells, images, index_ref, lower_ref, weight_ref, gaps, own, left, right, out, length):
    image = index_ref[0]
    from_left, of_other, of_own = mixing(CYCLES - 1, image, lower_ref, weight_ref)

    def write(other):
        for row in range(own.shape[0]):
            unfold(of_other * other[row] + of_own * own[row], out.at[row])

    @pl.when(from_left)
    def _():
        write(left)

    @pl.when(jnp.logical_not(from_left))
    def _():
        write(right)

    each = jnp.sum(gaps[...].reshape(images, -1, CYCLES, gaps.shape[-1]), axis=1)
    distance = jnp.sqrt(jnp.sum(each, axis=-1, keepdims=True) / cells + epsilon)
    position = lax.broadcasted_iota(jnp.int32, distance.shape, 0)
    reached = jnp.sum(jnp.where(position < image, distance, 0.0), axis=0)
    lane = lax.broadcasted_iota(jnp.int32, length.shape, 1)
    result = jnp.zeros(length.shape, jnp.float32)
    for cycle in range(CYCLES):
        result = jnp.where(lane == cycle, reached[cycle : cycle + 1], result)
    length[...] = result


def shaped(*shape):
    return jax.ShapeDtypeStruct(shape, jnp.float32)


def per_device(field, mobility, lower, weights):
    rows, depth, lanes = field.shape[1:]
    slab = (rows, depth // SUBLANES, SUBLANES, lanes)
    wide = (9 * rows,) + slab[1:]
    window = pltpu.VMEM(wide, jnp.float32)
    image_count, domain_count = lax.axis_size("image"), lax.axis_size("domain")
    image_index = lax.axis_index("image")[None]
    index = lax.axis_index("domain")
    lower, weights = lower.T, weights.T
    cells = rows * domain_count * depth * lanes

    packed = pl.pallas_call(
        pack_kernel,
        out_shape=shaped(2, *slab),
        in_specs=[pl.BlockSpec(memory_space=pltpu.HBM)] * 2,
        out_specs=VMEM,
        scratch_shapes=[
            pltpu.VMEM((2, rows, depth, lanes), jnp.float32),
            pltpu.SemaphoreType.DMA((2,)),
        ],
        compiler_params=PARAMS,
    )(field[0], mobility)
    phase, mobile = pl.pallas_call(
        first_kernel,
        out_shape=(shaped(*slab), shaped(*wide)),
        in_specs=[SMEM] + [VMEM] * 9,
        out_specs=(VMEM, VMEM),
        scratch_shapes=[window],
        compiler_params=PARAMS,
    )(index[None], *halo_pieces(packed, index))

    totals = []
    for cycle in range(CYCLES - 1):
        across = exchanged(phase, "image", lambda i, size: i - side(i, 1))
        inside = exchanged(phase, "image", partner_inside(1))
        phase, total = pl.pallas_call(
            lambda *refs, cycle=cycle: mix_kernel(cycle, *refs),
            out_shape=(shaped(*slab), shaped(1, lanes)),
            in_specs=[SMEM] * 3 + [VMEM] * 3,
            out_specs=(VMEM, VMEM),
            compiler_params=PARAMS,
        )(image_index, lower, weights, phase, inside, across)
        totals.append(total)
        phase = pl.pallas_call(
            later_kernel,
            out_shape=shaped(*slab),
            in_specs=[SMEM] + [VMEM] * 10,
            out_specs=VMEM,
            scratch_shapes=[window],
            compiler_params=PARAMS,
        )(index[None], *halo_pieces(phase, index), mobile)
    right, left = passed_along(phase, -1), passed_along(phase, 1)
    mine = pl.pallas_call(
        gap_kernel,
        out_shape=shaped(CYCLES, lanes),
        in_specs=[VMEM] * 3,
        out_specs=VMEM,
        compiler_params=PARAMS,
    )(phase, right, jnp.concatenate(totals, axis=0))
    everyone = jnp.broadcast_to(mine[None], (image_count * domain_count, CYCLES, lanes))
    gaps = lax.all_to_all(everyone, ("image", "domain"), 0, 0)
    evolved, arclength = pl.pallas_call(
        lambda *refs: last_kernel(cells, image_count, *refs),
        out_shape=(shaped(rows, depth, lanes), shaped(1, CYCLES)),
        in_specs=[SMEM] * 3 + [VMEM] * 4,
        out_specs=(VMEM, VMEM),
        compiler_params=PARAMS,
    )(image_index, lower, weights, gaps, phase, left, right)
    return evolved[None], arclength.T


def solution(mesh):
    return jax.shard_map(
        per_device,
        mesh=mesh,
        in_specs=(
            P("image", "domain", None, None),
            P("domain", None, None),
            P(None, "image"),
            P(None, "image"),
        ),
        out_specs=(P("image", "domain", None, None), P(None, "image")),
        check_vma=False,
    )
```

```python
import jax
import jax.numpy as jnp
from jax import lax
from jax.experimental import pallas as pl
from jax.experimental.pallas import tpu as pltpu
from jax.sharding import PartitionSpec as P

STEPS = 8
CYCLES = 2
SUBLANES = 8
UNROLL = 4

time_step = 0.008
epsilon = 1e-06

VMEM = pl.BlockSpec(memory_space=pltpu.VMEM)
SMEM = pl.BlockSpec(memory_space=pltpu.SMEM)
PARAMS = pltpu.CompilerParams(vmem_limit_bytes=16 << 20)


def exchanged(value, axis, partner):
    size = lax.axis_size(axis)
    pairs = [(i, partner(i, size)) for i in range(size)]
    return lax.ppermute(value, axis, [(i, j) for i, j in pairs if 0 <= j < size])


def passed_along(value, steps):
    count = lax.axis_size("image")
    first, last = (max(0, -steps), min(count, count - steps))
    return lax.ppermute(value, "image", [(i, i + steps) for i in range(first, last)])


def side(index, stride):
    return 1 - 2 * (index // stride % 2)


def partner_inside(stride):
    return lambda i, size: i + side(i, stride) * stride


def partner_across(stride):
    return lambda i, size: (i - side(i, stride) * stride) % size


def halo_pieces(own, index):
    straight = []
    for partner, stride in zip((partner_across, partner_inside) * 2, (2, 2, 4, 4)):
        straight.append(exchanged(own, "domain", partner(stride)))
    *twos, across, inside = straight
    chosen = jnp.where(side(index, 4) == side(index, 1), inside, across)
    beside = exchanged(own, "domain", partner_inside(1))
    others = [exchanged(piece, "domain", partner_inside(1)) for piece in (*twos, chosen)]
    return [own, *straight, beside, *others]


def slab_offsets(index):
    core, two, four = (side(index, stride) for stride in (1, 2, 4))
    straight = (0, -2 * two, 2 * two, -4 * four, 4 * four)
    return straight + (core, core - 2 * two, core + 2 * two, -3 * core)


def fill(window, index, pieces, rows):
    for offset, piece in zip(slab_offsets(index), pieces):
        start = pl.multiple_of((4 + offset) * rows, rows)
        window[pl.ds(start, rows)] = piece[...]


def fold(plane, target, place, scale=None):
    folds = target.shape[-3]
    for v in range(folds):
        part = plane[pl.ds(v, SUBLANES, stride=folds), :]
        target[(*place, v)] = part if scale is None else part * scale


def unfold(value, target):
    for v in range(value.shape[0]):
        target[pl.ds(v, SUBLANES, stride=value.shape[0]), :] = value[v]


def y_shifted(value, offset):
    if offset == 1:
        return jnp.concatenate([pltpu.roll(value[-1:], 1, 1), value[:-1]], axis=0)
    return jnp.concatenate([value[1:], pltpu.roll(value[:1], SUBLANES - 1, 1)], axis=0)


def z_shifted(value, offset):
    return pltpu.roll(value, offset % value.shape[2], 2)


def potential_and_motion(field, mobile, row):
    here = field[row]
    square = here * here
    around = field[row - 1] + field[row + 1]
    for shifted in (y_shifted, z_shifted):
        around = around + (shifted(here, 1) + shifted(here, -1))
    potential = here * (square + 5.0) - around
    motion = mobile[row] / (1.0 + square)
    return potential, motion


def take_steps(field, mobile, length):
    for step in range(STEPS):
        first, last = 2 * step + 2, length - 2 * step - 2
        before = potential_and_motion(field, mobile, first - 1)
        now = potential_and_motion(field, mobile, first)
        inflow = (before[1] + now[1]) * (now[0] - before[0])

        def one_row(row, carried):
            potential, motion, inflow = carried
            ahead = potential_and_motion(field, mobile, row + 1)
            outflow = (motion + ahead[1]) * (ahead[0] - potential)
            change = outflow - inflow
            for shifted in (y_shifted, z_shifted):
                flow = (motion + shifted(motion, 1)) * (potential - shifted(potential, 1))
                change = change + (shifted(flow, -1) - flow)
            field[row] = field[row] + change
            return ahead[0], ahead[1], outflow

        lax.fori_loop(first, last, one_row, (now[0], now[1], inflow), unroll=UNROLL)


def pack_kernel(field, mobility, out, held, semaphores):
    copies = [
        pltpu.make_async_copy(source, held.at[i], semaphores.at[i])
        for i, source in enumerate((field, mobility))
    ]
    for copy in copies:
        copy.start()
    for i, copy in enumerate(copies):
        copy.wait()
        for row in range(field.shape[0]):
            fold(held.at[i, row], out, (i, row), 0.5 * time_step if i else None)


def first_kernel(index_ref, *refs):
    pieces, out, mobile, window = refs[:9], *refs[9:]
    rows = out.shape[0]
    fill(window, index_ref[0], [piece.at[0] for piece in pieces], rows)
    fill(mobile, index_ref[0], [piece.at[1] for piece in pieces], rows)
    take_steps(window, mobile, 9 * rows)
    out[...] = window[pl.ds(4 * rows, rows)]


def later_kernel(index_ref, *refs):
    pieces, mobile, out, window = refs[:9], *refs[9:]
    rows = out.shape[0]
    fill(window, index_ref[0], pieces, rows)
    take_steps(window, mobile, 9 * rows)
    out[...] = window[pl.ds(4 * rows, rows)]


def squares_of(own, after):
    return jnp.sum(jnp.square(after[...] - own[...]), axis=(0, 1, 2))[None]


def mixing(cycle, image, lower_ref, weight_ref):
    from_left = lower_ref[0, cycle] < image
    weight = weight_ref[0, cycle]
    rest = 1.0 - weight
    return from_left, jnp.where(from_left, weight, rest), jnp.where(from_left, rest, weight)


def mix_kernel(cycle, index_ref, lower_ref, weight_ref, own, inside, across, out, total):
    image = index_ref[0]
    even = lax.rem(image, 2) == 0
    from_left, of_other, of_own = mixing(cycle, image, lower_ref, weight_ref)

    def when(condition, do, *refs):
        pl.when(condition)(lambda: do(*refs))

    def measure(after):
        total[...] = squares_of(own, after)

    def write(other):
        for row in range(own.shape[0]):
            out[row] = of_other * other[row] + of_own * own[row]

    when(even, measure, inside)
    when(jnp.logical_not(even), measure, across)
    when(from_left != even, write, inside)
    when(from_left == even, write, across)


def gap_kernel(own, right, earlier, total):
    total[: CYCLES - 1] = earlier[...]
    total[CYCLES - 1 :] = squares_of(own, right)


def last_kernel(cells, images, index_ref, lower_ref, weight_ref, gaps, own, left, right, out, length):
    image = index_ref[0]
    from_left, of_other, of_own = mixing(CYCLES - 1, image, lower_ref, weight_ref)

    def write(other):
        for row in range(own.shape[0]):
            unfold(of_other * other[row] + of_own * own[row], out.at[row])

    @pl.when(from_left)
    def _():
        write(left)

    @pl.when(jnp.logical_not(from_left))
    def _():
        write(right)

    each = jnp.sum(gaps[...].reshape(images, -1, CYCLES, gaps.shape[-1]), axis=1)
    distance = jnp.sqrt(jnp.sum(each, axis=-1, keepdims=True) / cells + epsilon)
    position = lax.broadcasted_iota(jnp.int32, distance.shape, 0)
    reached = jnp.sum(jnp.where(position < image, distance, 0.0), axis=0)
    lane = lax.broadcasted_iota(jnp.int32, length.shape, 1)
    result = jnp.zeros(length.shape, jnp.float32)
    for cycle in range(CYCLES):
        result = jnp.where(lane == cycle, reached[cycle : cycle + 1], result)
    length[...] = result


def shaped(*shape):
    return jax.ShapeDtypeStruct(shape, jnp.float32)


def cycles(field, mobility, lower, weights):
    rows, depth, lanes = field.shape[1:]
    slab = (rows, depth // SUBLANES, SUBLANES, lanes)
    wide = (9 * rows,) + slab[1:]
    window = pltpu.VMEM(wide, jnp.float32)
    image_count, domain_count = lax.axis_size("image"), lax.axis_size("domain")
    image_index = lax.axis_index("image")[None]
    index = lax.axis_index("domain")
    lower, weights = lower.T, weights.T
    cells = rows * domain_count * depth * lanes

    packed = pl.pallas_call(
        pack_kernel,
        out_shape=shaped(2, *slab),
        in_specs=[pl.BlockSpec(memory_space=pltpu.HBM)] * 2,
        out_specs=VMEM,
        scratch_shapes=[
            pltpu.VMEM((2, rows, depth, lanes), jnp.float32),
            pltpu.SemaphoreType.DMA((2,)),
        ],
        compiler_params=PARAMS,
    )(field[0], mobility)
    phase, mobile = pl.pallas_call(
        first_kernel,
        out_shape=(shaped(*slab), shaped(*wide)),
        in_specs=[SMEM] + [VMEM] * 9,
        out_specs=(VMEM, VMEM),
        scratch_shapes=[window],
        compiler_params=PARAMS,
    )(index[None], *halo_pieces(packed, index))

    totals = []
    for cycle in range(CYCLES - 1):
        across = exchanged(phase, "image", lambda i, size: i - side(i, 1))
        inside = exchanged(phase, "image", partner_inside(1))
        phase, total = pl.pallas_call(
            lambda *refs, cycle=cycle: mix_kernel(cycle, *refs),
            out_shape=(shaped(*slab), shaped(1, lanes)),
            in_specs=[SMEM] * 3 + [VMEM] * 3,
            out_specs=(VMEM, VMEM),
            compiler_params=PARAMS,
        )(image_index, lower, weights, phase, inside, across)
        totals.append(total)
        phase = pl.pallas_call(
            later_kernel,
            out_shape=shaped(*slab),
            in_specs=[SMEM] + [VMEM] * 10,
            out_specs=VMEM,
            scratch_shapes=[window],
            compiler_params=PARAMS,
        )(index[None], *halo_pieces(phase, index), mobile)
    right = passed_along(phase, -1)
    left = passed_along(phase, 1)
    mine = pl.pallas_call(
        gap_kernel,
        out_shape=shaped(CYCLES, lanes),
        in_specs=[VMEM] * 3,
        out_specs=VMEM,
        compiler_params=PARAMS,
    )(phase, right, jnp.concatenate(totals, axis=0))
    everyone = jnp.broadcast_to(mine[None], (image_count * domain_count, CYCLES, lanes))
    gaps = lax.all_to_all(everyone, ("image", "domain"), 0, 0)
    evolved, arclength = pl.pallas_call(
        lambda *refs: last_kernel(cells, image_count, *refs),
        out_shape=(shaped(rows, depth, lanes), shaped(1, CYCLES)),
        in_specs=[SMEM] * 3 + [VMEM] * 4,
        out_specs=(VMEM, VMEM),
        compiler_params=PARAMS,
    )(image_index, lower, weights, gaps, phase, left, right)
    return evolved[None], arclength.T


def solution(mesh):
    return jax.shard_map(
        cycles,
        mesh=mesh,
        in_specs=(
            P("image", "domain", None, None),
            P("domain", None, None),
            P(None, "image"),
            P(None, "image"),
        ),
        out_specs=(P("image", "domain", None, None), P(None, "image")),
        check_vma=False,
    )
```

```python
import jax
import jax.numpy as jnp
import numpy as np
from jax import lax
from jax.experimental import pallas as pl
from jax.experimental.pallas import tpu as pltpu
from jax.sharding import PartitionSpec as P

STEPS = 8
CYCLES = 2
SUBLANES = 8
UNROLL = 4
CHUNK = 8

time_step = 0.008
epsilon = 1e-06

VMEM = pl.BlockSpec(memory_space=pltpu.VMEM)
SMEM = pl.BlockSpec(memory_space=pltpu.SMEM)
PARAMS = pltpu.CompilerParams(vmem_limit_bytes=16 << 20)


def exchanged(value, axis, partner):
    size = lax.axis_size(axis)
    pairs = [(i, partner(i, size)) for i in range(size)]
    return lax.ppermute(value, axis, [(i, j) for i, j in pairs if 0 <= j < size])


def passed_along(value, steps):
    count = lax.axis_size("image")
    first, last = (max(0, -steps), min(count, count - steps))
    return lax.ppermute(value, "image", [(i, i + steps) for i in range(first, last)])


def side(index, stride):
    return 1 - 2 * (index // stride % 2)


def partner_inside(stride):
    return lambda i, size: i + side(i, stride) * stride


def partner_across(stride):
    return lambda i, size: (i - side(i, stride) * stride) % size


def halo_pieces(own, index):
    straight = []
    for partner, stride in zip((partner_across, partner_inside) * 2, (2, 2, 4, 4)):
        straight.append(exchanged(own, "domain", partner(stride)))
    *twos, across, inside = straight
    chosen = jnp.where(side(index, 4) == side(index, 1), inside, across)
    beside = exchanged(own, "domain", partner_inside(1))
    others = [exchanged(piece, "domain", partner_inside(1)) for piece in (*twos, chosen)]
    return [own, *straight, beside, *others]


def slab_offsets(index):
    core, two, four = (side(index, stride) for stride in (1, 2, 4))
    straight = (0, -2 * two, 2 * two, -4 * four, 4 * four)
    return straight + (core, core - 2 * two, core + 2 * two, -3 * core)


def fill(window, index, pieces, rows):
    for offset, piece in zip(slab_offsets(index), pieces):
        start = pl.multiple_of((4 + offset) * rows, rows)
        window[pl.ds(start, rows)] = piece[...]


def fold(plane, target, place, scale=None):
    folds = target.shape[-3]
    for v in range(folds):
        part = plane[pl.ds(v, SUBLANES, stride=folds), :]
        target[(*place, v)] = part if scale is None else part * scale


def unfold(value, target):
    for v in range(value.shape[0]):
        target[pl.ds(v, SUBLANES, stride=value.shape[0]), :] = value[v]


def y_shifted(value, offset):
    if offset == 1:
        return jnp.concatenate([pltpu.roll(value[-1:], 1, 1), value[:-1]], axis=0)
    return jnp.concatenate([value[1:], pltpu.roll(value[:1], SUBLANES - 1, 1)], axis=0)


def z_shifted(value, offset):
    return pltpu.roll(value, offset % value.shape[2], 2)


def z_neighbours(lanes):
    before = np.roll(np.eye(lanes), 1, axis=1)
    return jnp.asarray(np.tile(np.concatenate([before + before.T, before], axis=1), (2, 1)), jnp.bfloat16)


def gather(field, around, before, matrix, row, count):
    here = field[pl.ds(row, count)]
    lanes = here.shape[-1]
    flat = here.reshape(-1, lanes)
    high = flat.astype(jnp.bfloat16)
    low = (flat - high.astype(jnp.float32)).astype(jnp.bfloat16)
    found = jnp.dot(
        jnp.concatenate([high, low], axis=1), matrix[...], preferred_element_type=jnp.float32
    )
    around[pl.ds(row, count)] = found[:, :lanes].reshape(here.shape)
    before[pl.ds(row, count)] = found[:, lanes:].reshape(here.shape)


def take_steps(field, mobile, mobile_before, matrix, z_around, z_before, length):
    def at(row):
        here, before = field[row], z_before[row]
        square = here * here
        around = (field[row - 1] + field[row + 1]) + (y_shifted(here, 1) + y_shifted(here, -1))
        potential = here * (square + 5.0) - (around + z_around[row])
        motion = mobile[row] / (1.0 + square)
        return potential, motion, mobile_before[row] / (1.0 + before * before)

    def one_row(row, carried):
        potential, motion, motion_before, inflow = carried
        ahead = at(row + 1)
        outflow = (motion + ahead[1]) * (ahead[0] - potential)
        change = outflow - inflow
        flow = (motion + y_shifted(motion, 1)) * (potential - y_shifted(potential, 1))
        change = change + (y_shifted(flow, -1) - flow)
        flow = (motion + motion_before) * (potential - z_shifted(potential, 1))
        change = change + (z_shifted(flow, -1) - flow)
        field[row] = field[row] + change
        return (*ahead, outflow)

    for step in range(STEPS):
        first, last = 2 * step + 2, length - 2 * step - 2
        for row in range(first - 1, last + 1, CHUNK):
            gather(field, z_around, z_before, matrix, row, min(CHUNK, last + 1 - row))
        before, now = at(first - 1), at(first)
        inflow = (before[1] + now[1]) * (now[0] - before[0])
        lax.fori_loop(first, last, one_row, (*now, inflow), unroll=UNROLL)


def pack_kernel(field, mobility, out, held, semaphores):
    copies = [
        pltpu.make_async_copy(source, held.at[i], semaphores.at[i])
        for i, source in enumerate((field, mobility))
    ]
    for copy in copies:
        copy.start()
    for i, copy in enumerate(copies):
        copy.wait()
        for row in range(field.shape[0]):
            fold(held.at[i, row], out, (i, row), 0.5 * time_step if i else None)


def first_kernel(index_ref, *refs):
    pieces, matrix, out, mobile, mobile_before, *scratch = refs[:9], *refs[9:]
    window, rows = scratch[0], out.shape[0]
    fill(window, index_ref[0], [piece.at[0] for piece in pieces], rows)
    fill(mobile, index_ref[0], [piece.at[1] for piece in pieces], rows)

    def shift_row(row, carried):
        mobile_before[row] = z_shifted(mobile[row], 1)
        return carried

    lax.fori_loop(0, 9 * rows, shift_row, 0, unroll=UNROLL)
    take_steps(window, mobile, mobile_before, matrix, *scratch[1:], 9 * rows)
    out[...] = window[pl.ds(4 * rows, rows)]


def later_kernel(index_ref, *refs):
    pieces, mobile, mobile_before, matrix, out, *scratch = refs[:9], *refs[9:]
    window, rows = scratch[0], out.shape[0]
    fill(window, index_ref[0], pieces, rows)
    take_steps(window, mobile, mobile_before, matrix, *scratch[1:], 9 * rows)
    out[...] = window[pl.ds(4 * rows, rows)]


def squares_of(own, after):
    return jnp.sum(jnp.square(after[...] - own[...]), axis=(0, 1, 2))[None]


def mixing(cycle, image, lower_ref, weight_ref):
    from_left = lower_ref[0, cycle] < image
    weight = weight_ref[0, cycle]
    rest = 1.0 - weight
    return from_left, jnp.where(from_left, weight, rest), jnp.where(from_left, rest, weight)


def mix_kernel(cycle, index_ref, lower_ref, weight_ref, own, inside, across, out, total):
    image = index_ref[0]
    even = lax.rem(image, 2) == 0
    from_left, of_other, of_own = mixing(cycle, image, lower_ref, weight_ref)

    def when(condition, do, *refs):
        pl.when(condition)(lambda: do(*refs))

    def measure(after):
        total[...] = squares_of(own, after)

    def write(other):
        for row in range(own.shape[0]):
            out[row] = of_other * other[row] + of_own * own[row]

    when(even, measure, inside)
    when(jnp.logical_not(even), measure, across)
    when(from_left != even, write, inside)
    when(from_left == even, write, across)


def gap_kernel(own, right, *refs):
    *earlier, everyone = refs
    rows = [ref[...] for ref in earlier] + [squares_of(own, right)]
    for cycle, row in enumerate(rows):
        everyone[:, cycle : cycle + 1] = jnp.broadcast_to(row[None], (everyone.shape[0], *row.shape))


def final_mix_kernel(index_ref, lower_ref, weight_ref, own, left, right, out):
    from_left, of_other, of_own = mixing(CYCLES - 1, index_ref[0], lower_ref, weight_ref)

    def write(other):
        for row in range(own.shape[0]):
            unfold(of_other * other[row] + of_own * own[row], out.at[row])

    @pl.when(from_left)
    def _():
        write(left)

    @pl.when(jnp.logical_not(from_left))
    def _():
        write(right)


def length_kernel(cells, images, index_ref, gaps, length):
    each = jnp.sum(gaps[...].reshape(images, -1, CYCLES, gaps.shape[-1]), axis=1)
    distance = jnp.sqrt(jnp.sum(each, axis=-1, keepdims=True) / cells + epsilon)
    position = lax.broadcasted_iota(jnp.int32, distance.shape, 0)
    reached = jnp.sum(jnp.where(position < index_ref[0], distance, 0.0), axis=0)
    lane = lax.broadcasted_iota(jnp.int32, length.shape, 1)
    result = jnp.zeros(length.shape, jnp.float32)
    for cycle in range(CYCLES):
        result = jnp.where(lane == cycle, reached[cycle : cycle + 1], result)
    length[...] = result


def shaped(*shape):
    return jax.ShapeDtypeStruct(shape, jnp.float32)


def cycles(field, mobility, lower, weights):
    rows, depth, lanes = field.shape[1:]
    slab = (rows, depth // SUBLANES, SUBLANES, lanes)
    wide = (9 * rows,) + slab[1:]
    windows = [pltpu.VMEM(wide, jnp.float32)] * 3
    matrix = z_neighbours(lanes)
    image_count, domain_count = lax.axis_size("image"), lax.axis_size("domain")
    image_index = lax.axis_index("image")[None]
    index = lax.axis_index("domain")
    lower, weights = lower.T, weights.T
    cells = rows * domain_count * depth * lanes

    packed = pl.pallas_call(
        pack_kernel,
        out_shape=shaped(2, *slab),
        in_specs=[pl.BlockSpec(memory_space=pltpu.HBM)] * 2,
        out_specs=VMEM,
        scratch_shapes=[
            pltpu.VMEM((2, rows, depth, lanes), jnp.float32),
            pltpu.SemaphoreType.DMA((2,)),
        ],
        compiler_params=PARAMS,
    )(field[0], mobility)
    phase, *mobiles = pl.pallas_call(
        first_kernel,
        out_shape=(shaped(*slab), shaped(*wide), shaped(*wide)),
        in_specs=[SMEM] + [VMEM] * 10,
        out_specs=(VMEM, VMEM, VMEM),
        scratch_shapes=windows,
        compiler_params=PARAMS,
    )(index[None], *halo_pieces(packed, index), matrix)

    totals = []
    for cycle in range(CYCLES - 1):
        across = exchanged(phase, "image", lambda i, size: i - side(i, 1))
        inside = exchanged(phase, "image", partner_inside(1))
        phase, total = pl.pallas_call(
            lambda *refs, cycle=cycle: mix_kernel(cycle, *refs),
            out_shape=(shaped(*slab), shaped(1, lanes)),
            in_specs=[SMEM] * 3 + [VMEM] * 3,
            out_specs=(VMEM, VMEM),
            compiler_params=PARAMS,
        )(image_index, lower, weights, phase, inside, across)
        totals.append(total)
        phase = pl.pallas_call(
            later_kernel,
            out_shape=shaped(*slab),
            in_specs=[SMEM] + [VMEM] * 12,
            out_specs=VMEM,
            scratch_shapes=windows,
            compiler_params=PARAMS,
        )(index[None], *halo_pieces(phase, index), *mobiles, matrix)
    right = passed_along(phase, -1)
    left = passed_along(phase, 1)
    everyone = pl.pallas_call(
        gap_kernel,
        out_shape=shaped(image_count * domain_count, CYCLES, lanes),
        in_specs=[VMEM] * (2 + len(totals)),
        out_specs=VMEM,
        compiler_params=PARAMS,
    )(phase, right, *totals)
    gaps = lax.all_to_all(everyone, ("image", "domain"), 0, 0)
    evolved = pl.pallas_call(
        final_mix_kernel,
        out_shape=shaped(rows, depth, lanes),
        in_specs=[SMEM] * 3 + [VMEM] * 3,
        out_specs=VMEM,
        compiler_params=PARAMS,
    )(image_index, lower, weights, phase, left, right)
    arclength = pl.pallas_call(
        lambda *refs: length_kernel(cells, image_count, *refs),
        out_shape=shaped(1, CYCLES),
        in_specs=[SMEM, VMEM],
        out_specs=VMEM,
        compiler_params=PARAMS,
    )(image_index, gaps)
    return evolved[None], arclength.T


def solution(mesh):
    return jax.shard_map(
        cycles,
        mesh=mesh,
        in_specs=(
            P("image", "domain", None, None),
            P("domain", None, None),
            P(None, "image"),
            P(None, "image"),
        ),
        out_specs=(P("image", "domain", None, None), P(None, "image")),
        check_vma=False,
    )
```

```python
import jax
import jax.numpy as jnp
from jax import lax
from jax.experimental import pallas as pl
from jax.experimental.pallas import tpu as pltpu
from jax.sharding import PartitionSpec as P

STEPS = 8
CYCLES = 2
SUBLANES = 8
UNROLL = 4
CHUNK = 8

time_step = 0.008
epsilon = 1e-06

VMEM = pl.BlockSpec(memory_space=pltpu.VMEM)
SMEM = pl.BlockSpec(memory_space=pltpu.SMEM)
PARAMS = pltpu.CompilerParams(vmem_limit_bytes=16 << 20)


def exchanged(value, axis, partner):
    size = lax.axis_size(axis)
    pairs = [(i, partner(i, size)) for i in range(size)]
    return lax.ppermute(value, axis, [(i, j) for i, j in pairs if 0 <= j < size])


def passed_along(value, steps):
    count = lax.axis_size("image")
    first, last = (max(0, -steps), min(count, count - steps))
    return lax.ppermute(value, "image", [(i, i + steps) for i in range(first, last)])


def side(index, stride):
    return 1 - 2 * (index // stride % 2)


def partner_inside(stride):
    return lambda i, size: i + side(i, stride) * stride


def partner_across(stride):
    return lambda i, size: (i - side(i, stride) * stride) % size


def halo_pieces(own, index):
    straight = []
    for partner, stride in zip((partner_across, partner_inside) * 2, (2, 2, 4, 4)):
        straight.append(exchanged(own, "domain", partner(stride)))
    *twos, across, inside = straight
    chosen = jnp.where(side(index, 4) == side(index, 1), inside, across)
    beside = exchanged(own, "domain", partner_inside(1))
    others = [exchanged(piece, "domain", partner_inside(1)) for piece in (*twos, chosen)]
    return [own, *straight, beside, *others]


def slab_offsets(index):
    core, two, four = (side(index, stride) for stride in (1, 2, 4))
    straight = (0, -2 * two, 2 * two, -4 * four, 4 * four)
    return straight + (core, core - 2 * two, core + 2 * two, -3 * core)


def fill(window, index, pieces, rows):
    for offset, piece in zip(slab_offsets(index), pieces):
        start = pl.multiple_of((4 + offset) * rows, rows)
        window[pl.ds(start, rows)] = piece[...]


def fold(plane, target, place, scale=None):
    folds = target.shape[-3]
    for v in range(folds):
        part = plane[pl.ds(v, SUBLANES, stride=folds), :]
        target[(*place, v)] = part if scale is None else part * scale


def unfold(value, target):
    for v in range(value.shape[0]):
        target[pl.ds(v, SUBLANES, stride=value.shape[0]), :] = value[v]


def y_shifted(value, offset):
    if offset == 1:
        return jnp.concatenate([pltpu.roll(value[-1:], 1, 1), value[:-1]], axis=0)
    return jnp.concatenate([value[1:], pltpu.roll(value[:1], SUBLANES - 1, 1)], axis=0)


def z_shifted(value, offset):
    return pltpu.roll(value, offset % value.shape[2], 2)


def z_neighbours(lanes):
    shape = (2 * lanes, 2 * lanes)
    source = lax.rem(lax.broadcasted_iota(jnp.int32, shape, 0), lanes)
    column = lax.broadcasted_iota(jnp.int32, shape, 1)
    ahead = lax.rem(lax.rem(column, lanes) - source + lanes, lanes)
    before = jnp.where(ahead == 1, 1.0, 0.0)
    after = jnp.where(ahead == lanes - 1, 1.0, 0.0) * jnp.where(column < lanes, 1.0, 0.0)
    return (before + after).astype(jnp.bfloat16)


def gather(field, around, before, matrix, row, count):
    here = field[pl.ds(row, count)]
    lanes = here.shape[-1]
    flat = here.reshape(-1, lanes)
    high = flat.astype(jnp.bfloat16)
    low = (flat - high.astype(jnp.float32)).astype(jnp.bfloat16)
    found = jnp.dot(
        jnp.concatenate([high, low], axis=1), matrix[...], preferred_element_type=jnp.float32
    )
    around[pl.ds(row, count)] = found[:, :lanes].reshape(here.shape)
    before[pl.ds(row, count)] = found[:, lanes:].reshape(here.shape)


def take_steps(field, mobile, mobile_before, matrix, z_around, z_before, length):
    matrix[...] = z_neighbours(field.shape[-1])

    def shift_row(row, carried):
        mobile_before[row] = z_shifted(mobile[row], 1)
        return carried

    lax.fori_loop(0, length, shift_row, 0, unroll=UNROLL)

    def at(row):
        here, before = field[row], z_before[row]
        square = here * here
        around = (field[row - 1] + field[row + 1]) + (y_shifted(here, 1) + y_shifted(here, -1))
        potential = here * (square + 5.0) - (around + z_around[row])
        motion = mobile[row] / (1.0 + square)
        return potential, motion, mobile_before[row] / (1.0 + before * before)

    def one_row(row, carried):
        potential, motion, motion_before, inflow = carried
        ahead = at(row + 1)
        outflow = (motion + ahead[1]) * (ahead[0] - potential)
        change = outflow - inflow
        flow = (motion + y_shifted(motion, 1)) * (potential - y_shifted(potential, 1))
        change = change + (y_shifted(flow, -1) - flow)
        flow = (motion + motion_before) * (potential - z_shifted(potential, 1))
        change = change + (z_shifted(flow, -1) - flow)
        field[row] = field[row] + change
        return (*ahead, outflow)

    for step in range(STEPS):
        first, last = 2 * step + 2, length - 2 * step - 2
        for row in range(first - 1, last + 1, CHUNK):
            gather(field, z_around, z_before, matrix, row, min(CHUNK, last + 1 - row))
        before, now = at(first - 1), at(first)
        inflow = (before[1] + now[1]) * (now[0] - before[0])
        lax.fori_loop(first, last, one_row, (*now, inflow), unroll=UNROLL)


def pack_kernel(field, mobility, out, held, semaphores):
    copies = [
        pltpu.make_async_copy(source, held.at[i], semaphores.at[i])
        for i, source in enumerate((field, mobility))
    ]
    for copy in copies:
        copy.start()
    for i, copy in enumerate(copies):
        copy.wait()
        for row in range(field.shape[0]):
            fold(held.at[i, row], out, (i, row), 0.5 * time_step if i else None)


def first_kernel(index_ref, *refs):
    pieces, out, mobile, window, *scratch = refs[:9], *refs[9:]
    rows = out.shape[0]
    fill(window, index_ref[0], [piece.at[0] for piece in pieces], rows)
    fill(mobile, index_ref[0], [piece.at[1] for piece in pieces], rows)

    take_steps(window, mobile, *scratch, 9 * rows)
    out[...] = window[pl.ds(4 * rows, rows)]


def later_kernel(index_ref, *refs):
    pieces, mobile, out, window, *scratch = refs[:9], *refs[9:]
    rows = out.shape[0]
    fill(window, index_ref[0], pieces, rows)
    take_steps(window, mobile, *scratch, 9 * rows)
    out[...] = window[pl.ds(4 * rows, rows)]


def squares_of(own, after):
    return jnp.sum(jnp.square(after[...] - own[...]), axis=(0, 1, 2))[None]


def mixing(cycle, image, lower_ref, weight_ref):
    from_left = lower_ref[0, cycle] < image
    weight = weight_ref[0, cycle]
    rest = 1.0 - weight
    return from_left, jnp.where(from_left, weight, rest), jnp.where(from_left, rest, weight)


def mix_kernel(cycle, index_ref, lower_ref, weight_ref, own, inside, across, out, total):
    image = index_ref[0]
    even = lax.rem(image, 2) == 0
    from_left, of_other, of_own = mixing(cycle, image, lower_ref, weight_ref)

    def when(condition, do, *refs):
        pl.when(condition)(lambda: do(*refs))

    def measure(after):
        total[...] = squares_of(own, after)

    def write(other):
        for row in range(own.shape[0]):
            out[row] = of_other * other[row] + of_own * own[row]

    when(even, measure, inside)
    when(jnp.logical_not(even), measure, across)
    when(from_left != even, write, inside)
    when(from_left == even, write, across)


def gap_kernel(own, right, *refs):
    *earlier, everyone = refs
    rows = [ref[...] for ref in earlier] + [squares_of(own, right)]
    for cycle, row in enumerate(rows):
        everyone[:, cycle : cycle + 1] = jnp.broadcast_to(row[None], (everyone.shape[0], *row.shape))


def final_mix_kernel(index_ref, lower_ref, weight_ref, own, left, right, out):
    from_left, of_other, of_own = mixing(CYCLES - 1, index_ref[0], lower_ref, weight_ref)

    def write(other):
        for row in range(own.shape[0]):
            unfold(of_other * other[row] + of_own * own[row], out.at[row])

    @pl.when(from_left)
    def _():
        write(left)

    @pl.when(jnp.logical_not(from_left))
    def _():
        write(right)


def length_kernel(cells, images, index_ref, gaps, length):
    each = jnp.sum(gaps[...].reshape(images, -1, CYCLES, gaps.shape[-1]), axis=1)
    distance = jnp.sqrt(jnp.sum(each, axis=-1, keepdims=True) / cells + epsilon)
    position = lax.broadcasted_iota(jnp.int32, distance.shape, 0)
    reached = jnp.sum(jnp.where(position < index_ref[0], distance, 0.0), axis=0)
    lane = lax.broadcasted_iota(jnp.int32, length.shape, 1)
    result = jnp.zeros(length.shape, jnp.float32)
    for cycle in range(CYCLES):
        result = jnp.where(lane == cycle, reached[cycle : cycle + 1], result)
    length[...] = result


def shaped(*shape):
    return jax.ShapeDtypeStruct(shape, jnp.float32)


def cycles(field, mobility, lower, weights):
    rows, depth, lanes = field.shape[1:]
    slab = (rows, depth // SUBLANES, SUBLANES, lanes)
    wide = (9 * rows,) + slab[1:]
    windows = [pltpu.VMEM(wide, jnp.float32)] * 2
    windows += [pltpu.VMEM((2 * lanes, 2 * lanes), jnp.bfloat16)]
    windows += [pltpu.VMEM(wide, jnp.float32)] * 2
    image_count, domain_count = lax.axis_size("image"), lax.axis_size("domain")
    image_index = lax.axis_index("image")[None]
    index = lax.axis_index("domain")
    lower, weights = lower.T, weights.T
    cells = rows * domain_count * depth * lanes

    packed = pl.pallas_call(
        pack_kernel,
        out_shape=shaped(2, *slab),
        in_specs=[pl.BlockSpec(memory_space=pltpu.HBM)] * 2,
        out_specs=VMEM,
        scratch_shapes=[
            pltpu.VMEM((2, rows, depth, lanes), jnp.float32),
            pltpu.SemaphoreType.DMA((2,)),
        ],
        compiler_params=PARAMS,
    )(field[0], mobility)
    phase, mobile = pl.pallas_call(
        first_kernel,
        out_shape=(shaped(*slab), shaped(*wide)),
        in_specs=[SMEM] + [VMEM] * 9,
        out_specs=(VMEM,) * 2,
        scratch_shapes=windows,
        compiler_params=PARAMS,
    )(index[None], *halo_pieces(packed, index))

    totals = []
    for cycle in range(CYCLES - 1):
        across = exchanged(phase, "image", lambda i, size: i - side(i, 1))
        inside = exchanged(phase, "image", partner_inside(1))
        phase, total = pl.pallas_call(
            lambda *refs, cycle=cycle: mix_kernel(cycle, *refs),
            out_shape=(shaped(*slab), shaped(1, lanes)),
            in_specs=[SMEM] * 3 + [VMEM] * 3,
            out_specs=(VMEM, VMEM),
            compiler_params=PARAMS,
        )(image_index, lower, weights, phase, inside, across)
        totals.append(total)
        phase = pl.pallas_call(
            later_kernel,
            out_shape=shaped(*slab),
            in_specs=[SMEM] + [VMEM] * 10,
            out_specs=VMEM,
            scratch_shapes=windows,
            compiler_params=PARAMS,
        )(index[None], *halo_pieces(phase, index), mobile)
    right = passed_along(phase, -1)
    left = passed_along(phase, 1)
    everyone = pl.pallas_call(
        gap_kernel,
        out_shape=shaped(image_count * domain_count, CYCLES, lanes),
        in_specs=[VMEM] * (2 + len(totals)),
        out_specs=VMEM,
        compiler_params=PARAMS,
    )(phase, right, *totals)
    gaps = lax.all_to_all(everyone, ("image", "domain"), 0, 0)
    evolved = pl.pallas_call(
        final_mix_kernel,
        out_shape=shaped(rows, depth, lanes),
        in_specs=[SMEM] * 3 + [VMEM] * 3,
        out_specs=VMEM,
        compiler_params=PARAMS,
    )(image_index, lower, weights, phase, left, right)
    arclength = pl.pallas_call(
        lambda *refs: length_kernel(cells, image_count, *refs),
        out_shape=shaped(1, CYCLES),
        in_specs=[SMEM, VMEM],
        out_specs=VMEM,
        compiler_params=PARAMS,
    )(image_index, gaps)
    return evolved[None], arclength.T


def solution(mesh):
    return jax.shard_map(
        cycles,
        mesh=mesh,
        in_specs=(
            P("image", "domain", None, None),
            P("domain", None, None),
            P(None, "image"),
            P(None, "image"),
        ),
        out_specs=(P("image", "domain", None, None), P(None, "image")),
        check_vma=False,
    )
```

```python
import jax
import jax.numpy as jnp
from jax import lax
from jax.experimental import pallas as pl
from jax.experimental.pallas import tpu as pltpu
from jax.sharding import PartitionSpec as P

STEPS = 8
CYCLES = 2
SUBLANES = 8
UNROLL = 4
CHUNK = 8

time_step = 0.008
epsilon = 1e-06

VMEM = pl.BlockSpec(memory_space=pltpu.VMEM)
SMEM = pl.BlockSpec(memory_space=pltpu.SMEM)
HBM = pl.BlockSpec(memory_space=pltpu.HBM)
PARAMS = pltpu.CompilerParams(vmem_limit_bytes=16 << 20)


def exchanged(value, axis, partner):
    size = lax.axis_size(axis)
    pairs = [(i, partner(i, size)) for i in range(size)]
    return lax.ppermute(value, axis, [(i, j) for i, j in pairs if 0 <= j < size])


def passed_along(value, steps):
    count = lax.axis_size("image")
    first, last = (max(0, -steps), min(count, count - steps))
    return lax.ppermute(value, "image", [(i, i + steps) for i in range(first, last)])


def side(index, stride):
    return 1 - 2 * (index // stride % 2)


def partner_inside(stride):
    return lambda i, size: i + side(i, stride) * stride


def partner_across(stride):
    return lambda i, size: (i - side(i, stride) * stride) % size


def halo_pieces(own, index):
    straight = []
    for partner, stride in zip((partner_across, partner_inside) * 2, (2, 2, 4, 4)):
        straight.append(exchanged(own, "domain", partner(stride)))
    *twos, across, inside = straight
    chosen = jnp.where(side(index, 4) == side(index, 1), inside, across)
    beside = exchanged(own, "domain", partner_inside(1))
    others = [exchanged(piece, "domain", partner_inside(1)) for piece in (*twos, chosen)]
    return [own, *straight, beside, *others]


def slab_offsets(index):
    core, two, four = (side(index, stride) for stride in (1, 2, 4))
    straight = (0, -2 * two, 2 * two, -4 * four, 4 * four)
    return straight + (core, core - 2 * two, core + 2 * two, -3 * core)


def fill(window, index, pieces, rows):
    for offset, piece in zip(slab_offsets(index), pieces):
        start = pl.multiple_of((4 + offset) * rows, rows)
        window[pl.ds(start, rows)] = piece[...]


def fold(plane, target, place, scale=None):
    folds = target.shape[-3]
    for v in range(folds):
        part = plane[pl.ds(v, SUBLANES, stride=folds), :]
        target[(*place, v)] = part if scale is None else part * scale


def unfold(value, target):
    for v in range(value.shape[0]):
        target[pl.ds(v, SUBLANES, stride=value.shape[0]), :] = value[v]


def y_shifted(value, offset):
    if offset == 1:
        return jnp.concatenate([pltpu.roll(value[-1:], 1, 1), value[:-1]], axis=0)
    return jnp.concatenate([value[1:], pltpu.roll(value[:1], SUBLANES - 1, 1)], axis=0)


def z_shifted(value, offset):
    return pltpu.roll(value, offset % value.shape[2], 2)


def z_neighbours(lanes):
    shape = (2 * lanes, 2 * lanes)
    source = lax.rem(lax.broadcasted_iota(jnp.int32, shape, 0), lanes)
    column = lax.broadcasted_iota(jnp.int32, shape, 1)
    ahead = lax.rem(lax.rem(column, lanes) - source + lanes, lanes)
    before = jnp.where(ahead == 1, 1.0, 0.0)
    after = jnp.where(ahead == lanes - 1, 1.0, 0.0) * jnp.where(column < lanes, 1.0, 0.0)
    return (before + after).astype(jnp.bfloat16)


def gather(field, around, before, matrix, row, count):
    here = field[pl.ds(row, count)]
    lanes = here.shape[-1]
    flat = here.reshape(-1, lanes)
    high = flat.astype(jnp.bfloat16)
    low = (flat - high.astype(jnp.float32)).astype(jnp.bfloat16)
    found = jnp.dot(
        jnp.concatenate([high, low], axis=1), matrix[...], preferred_element_type=jnp.float32
    )
    around[pl.ds(row, count)] = found[:, :lanes].reshape(here.shape)
    before[pl.ds(row, count)] = found[:, lanes:].reshape(here.shape)


def take_steps(field, mobile, mobile_before, matrix, z_around, z_before, length):
    matrix[...] = z_neighbours(field.shape[-1])

    def at(row):
        here, before = field[row], z_before[row]
        square = here * here
        around = (field[row - 1] + field[row + 1]) + (y_shifted(here, 1) + y_shifted(here, -1))
        potential = here * (square + 5.0) - (around + z_around[row])
        motion = mobile[row] / (1.0 + square)
        return potential, motion, mobile_before[row] / (1.0 + before * before)

    def one_row(row, carried):
        potential, motion, motion_before, inflow = carried
        ahead = at(row + 1)
        outflow = (motion + ahead[1]) * (ahead[0] - potential)
        change = outflow - inflow
        flow = (motion + y_shifted(motion, 1)) * (potential - y_shifted(potential, 1))
        change = change + (y_shifted(flow, -1) - flow)
        flow = (motion + motion_before) * (potential - z_shifted(potential, 1))
        change = change + (z_shifted(flow, -1) - flow)
        field[row] = field[row] + change
        return (*ahead, outflow)

    for step in range(STEPS):
        first, last = 2 * step + 2, length - 2 * step - 2
        for row in range(first - 1, last + 1, CHUNK):
            gather(field, z_around, z_before, matrix, row, min(CHUNK, last + 1 - row))
        before, now = at(first - 1), at(first)
        inflow = (before[1] + now[1]) * (now[0] - before[0])
        lax.fori_loop(first, last, one_row, (*now, inflow), unroll=UNROLL)


def pack_kernel(field, mobility, out, held, semaphores):
    copies = [
        pltpu.make_async_copy(source, held.at[i], semaphores.at[i])
        for i, source in enumerate((field, mobility))
    ]
    for copy in copies:
        copy.start()
    for i, copy in enumerate(copies):
        copy.wait()
        for row in range(field.shape[0]):
            fold(held.at[i, row], out, (i, row), 0.5 * time_step if i else None)


def shift_kernel(mobile, mobile_before):
    def shift_row(row, carried):
        mobile_before[row] = z_shifted(mobile[row], 1)
        return carried

    lax.fori_loop(0, mobile.shape[0], shift_row, 0, unroll=UNROLL)


def first_kernel(index_ref, *refs):
    pieces, out, mobile, window, mobile_before, *scratch = refs[:9], *refs[9:]
    rows = out.shape[0]
    fill(window, index_ref[0], [piece.at[0] for piece in pieces], rows)
    fill(mobile, index_ref[0], [piece.at[1] for piece in pieces], rows)
    shift_kernel(mobile, mobile_before)
    take_steps(window, mobile, mobile_before, *scratch, 9 * rows)
    out[...] = window[pl.ds(4 * rows, rows)]


def later_kernel(index_ref, *refs):
    pieces, mobile, mobile_before, out, window, *scratch = refs[:9], *refs[9:]
    rows = out.shape[0]
    fill(window, index_ref[0], pieces, rows)
    take_steps(window, mobile, mobile_before, *scratch, 9 * rows)
    out[...] = window[pl.ds(4 * rows, rows)]


def squares_of(own, after):
    return jnp.sum(jnp.square(after[...] - own[...]), axis=(0, 1, 2))[None]


def mixing(cycle, image, lower_ref, weight_ref):
    from_left = lower_ref[0, cycle] < image
    weight = weight_ref[0, cycle]
    rest = 1.0 - weight
    return from_left, jnp.where(from_left, weight, rest), jnp.where(from_left, rest, weight)


def mix_kernel(cycle, index_ref, lower_ref, weight_ref, own, inside, across, out, total):
    image = index_ref[0]
    even = lax.rem(image, 2) == 0
    from_left, of_other, of_own = mixing(cycle, image, lower_ref, weight_ref)

    def when(condition, do, *refs):
        pl.when(condition)(lambda: do(*refs))

    def measure(after):
        total[...] = squares_of(own, after)

    def write(other):
        for row in range(own.shape[0]):
            out[row] = of_other * other[row] + of_own * own[row]

    when(even, measure, inside)
    when(jnp.logical_not(even), measure, across)
    when(from_left != even, write, inside)
    when(from_left == even, write, across)


def halves(rows):
    lanes = rows[0].shape[-1]
    lane = lax.broadcasted_iota(jnp.int32, rows[0].shape, 1)
    first, second = (row + pltpu.roll(row, lanes // 2, 1) for row in rows)
    return jnp.where(lane < lanes // 2, first, second)


def gap_kernel(own, right, earlier, everyone):
    row = halves((earlier[...], squares_of(own, right)))
    everyone[...] = jnp.broadcast_to(row[None], everyone.shape)


def final_mix_kernel(index_ref, lower_ref, weight_ref, own, left, right, out):
    from_left, of_other, of_own = mixing(CYCLES - 1, index_ref[0], lower_ref, weight_ref)

    def write(other):
        for row in range(own.shape[0]):
            unfold(of_other * other[row] + of_own * own[row], out.at[row])

    @pl.when(from_left)
    def _():
        write(left)

    @pl.when(jnp.logical_not(from_left))
    def _():
        write(right)


def length_kernel(cells, images, index_ref, gaps, length):
    lanes = gaps.shape[-1]
    each = jnp.sum(gaps[...].reshape(images, -1, lanes), axis=1)
    early = lax.broadcasted_iota(jnp.int32, each.shape, 1) < lanes // 2
    position = lax.broadcasted_iota(jnp.int32, each.shape, 0)
    lane = lax.broadcasted_iota(jnp.int32, length.shape, 1)
    result = jnp.zeros(length.shape, jnp.float32)
    for cycle, chosen in enumerate((early, jnp.logical_not(early))):
        total = jnp.sum(jnp.where(chosen, each, 0.0), axis=1, keepdims=True)
        distance = jnp.sqrt(total / cells + epsilon)
        reached = jnp.sum(jnp.where(position[:, :1] < index_ref[0], distance, 0.0), axis=0, keepdims=True)
        result = jnp.where(lane == cycle, reached, result)
    length[...] = result


def shaped(*shape):
    return jax.ShapeDtypeStruct(shape, jnp.float32)


def cycles(field, mobility, lower, weights):
    rows, depth, lanes = field.shape[1:]
    slab = (rows, depth // SUBLANES, SUBLANES, lanes)
    wide = (9 * rows,) + slab[1:]
    window = [pltpu.VMEM(wide, jnp.float32)]
    scratch = [pltpu.VMEM((2 * lanes, 2 * lanes), jnp.bfloat16), *window, *window]
    image_count, domain_count = lax.axis_size("image"), lax.axis_size("domain")
    image_index = lax.axis_index("image")[None]
    index = lax.axis_index("domain")
    lower, weights = lower.T, weights.T
    cells = rows * domain_count * depth * lanes

    packed = pl.pallas_call(
        pack_kernel,
        out_shape=shaped(2, *slab),
        in_specs=[HBM] * 2,
        out_specs=VMEM,
        scratch_shapes=[
            pltpu.VMEM((2, rows, depth, lanes), jnp.float32),
            pltpu.SemaphoreType.DMA((2,)),
        ],
        compiler_params=PARAMS,
    )(field[0], mobility)
    phase, mobile = pl.pallas_call(
        first_kernel,
        out_shape=(shaped(*slab), shaped(*wide)),
        in_specs=[SMEM] + [VMEM] * 9,
        out_specs=(VMEM, VMEM),
        scratch_shapes=[*window, *window, *scratch],
        compiler_params=PARAMS,
    )(index[None], *halo_pieces(packed, index))
    mobile_before = pl.pallas_call(
        shift_kernel,
        out_shape=shaped(*wide),
        in_specs=[VMEM],
        out_specs=VMEM,
        compiler_params=PARAMS,
    )(mobile)

    totals = []
    for cycle in range(CYCLES - 1):
        across = exchanged(phase, "image", lambda i, size: i - side(i, 1))
        inside = exchanged(phase, "image", partner_inside(1))
        phase, total = pl.pallas_call(
            lambda *refs, cycle=cycle: mix_kernel(cycle, *refs),
            out_shape=(shaped(*slab), shaped(1, lanes)),
            in_specs=[SMEM] * 3 + [VMEM] * 3,
            out_specs=(VMEM, VMEM),
            compiler_params=PARAMS,
        )(image_index, lower, weights, phase, inside, across)
        totals.append(total)
        phase = pl.pallas_call(
            later_kernel,
            out_shape=shaped(*slab),
            in_specs=[SMEM] + [VMEM] * 11,
            out_specs=VMEM,
            scratch_shapes=[*window, *scratch],
            compiler_params=PARAMS,
        )(index[None], *halo_pieces(phase, index), mobile, mobile_before)
    right = passed_along(phase, -1)
    left = passed_along(phase, 1)
    everyone = pl.pallas_call(
        gap_kernel,
        out_shape=shaped(image_count * domain_count, 1, lanes),
        in_specs=[VMEM] * 3,
        out_specs=VMEM,
        compiler_params=PARAMS,
    )(phase, right, *totals)
    gaps = lax.all_to_all(everyone, ("image", "domain"), 0, 0)
    evolved = pl.pallas_call(
        final_mix_kernel,
        out_shape=shaped(rows, depth, lanes),
        in_specs=[SMEM] * 3 + [VMEM] * 3,
        out_specs=VMEM,
        compiler_params=PARAMS,
    )(image_index, lower, weights, phase, left, right)
    arclength = pl.pallas_call(
        lambda *refs: length_kernel(cells, image_count, *refs),
        out_shape=shaped(1, CYCLES),
        in_specs=[SMEM, VMEM],
        out_specs=VMEM,
        compiler_params=PARAMS,
    )(image_index, gaps)
    return evolved[None], arclength.T


def solution(mesh):
    return jax.shard_map(
        cycles,
        mesh=mesh,
        in_specs=(
            P("image", "domain", None, None),
            P("domain", None, None),
            P(None, "image"),
            P(None, "image"),
        ),
        out_specs=(P("image", "domain", None, None), P(None, "image")),
        check_vma=False,
    )
```

```python
import jax
import jax.numpy as jnp
from jax import lax
from jax.experimental import pallas as pl
from jax.experimental.pallas import tpu as pltpu
from jax.sharding import PartitionSpec as P

STEPS = 8
CYCLES = 2
SUBLANES = 8
UNROLL = 4
CHUNK = 8

time_step = 0.008
epsilon = 1e-06

VMEM = pl.BlockSpec(memory_space=pltpu.VMEM)
SMEM = pl.BlockSpec(memory_space=pltpu.SMEM)
HBM = pl.BlockSpec(memory_space=pltpu.HBM)
PARAMS = pltpu.CompilerParams(vmem_limit_bytes=16 << 20)


def exchanged(value, axis, partner):
    size = lax.axis_size(axis)
    pairs = [(i, partner(i, size)) for i in range(size)]
    return lax.ppermute(value, axis, [(i, j) for i, j in pairs if 0 <= j < size])


def passed_along(value, steps):
    count = lax.axis_size("image")
    first, last = (max(0, -steps), min(count, count - steps))
    return lax.ppermute(value, "image", [(i, i + steps) for i in range(first, last)])


def side(index, stride):
    return 1 - 2 * (index // stride % 2)


def partner_inside(stride):
    return lambda i, size: i + side(i, stride) * stride


def partner_across(stride):
    return lambda i, size: (i - side(i, stride) * stride) % size


CORE_STARTS = ("core_inside_two", "core_across_two", "core_chosen")


def halo_pieces(own, index):
    straight = []
    for partner, stride in zip((partner_across, partner_inside) * 2, (2, 2, 4, 4)):
        straight.append(exchanged(own, "domain", partner(stride)))
    across_two, inside_two, across, inside = straight
    beside = exchanged(own, "domain", partner_inside(1))
    others = {}
    for name, piece in zip(CORE_STARTS[:2], (inside_two, across_two)):
        others[name] = exchanged(piece, "domain", partner_inside(1))
    chosen = jnp.where(side(index, 4) == side(index, 1), inside, across)
    last = exchanged(chosen, "domain", partner_inside(1))
    return [own, *straight, beside, others[CORE_STARTS[1]], others[CORE_STARTS[0]], last]


def slab_offsets(index):
    core, two, four = (side(index, stride) for stride in (1, 2, 4))
    straight = (0, -2 * two, 2 * two, -4 * four, 4 * four)
    return straight + (core, core - 2 * two, core + 2 * two, -3 * core)


def fill(window, index, pieces, rows):
    for offset, piece in zip(slab_offsets(index), pieces):
        start = pl.multiple_of((4 + offset) * rows, rows)
        window[pl.ds(start, rows)] = piece[...]


def fold(plane, target, place, scale=None):
    folds = target.shape[-3]
    for v in range(folds):
        part = plane[pl.ds(v, SUBLANES, stride=folds), :]
        target[(*place, v)] = part if scale is None else part * scale


def unfold(value, target):
    for v in range(value.shape[0]):
        target[pl.ds(v, SUBLANES, stride=value.shape[0]), :] = value[v]


def y_shifted(value, offset):
    if offset == 1:
        return jnp.concatenate([pltpu.roll(value[-1:], 1, 1), value[:-1]], axis=0)
    return jnp.concatenate([value[1:], pltpu.roll(value[:1], SUBLANES - 1, 1)], axis=0)


def z_shifted(value, offset):
    return pltpu.roll(value, offset % value.shape[2], 2)


def z_neighbours(lanes):
    shape = (2 * lanes, 2 * lanes)
    source = lax.rem(lax.broadcasted_iota(jnp.int32, shape, 0), lanes)
    column = lax.broadcasted_iota(jnp.int32, shape, 1)
    ahead = lax.rem(lax.rem(column, lanes) - source + lanes, lanes)
    before = jnp.where(ahead == 1, 1.0, 0.0)
    after = jnp.where(ahead == lanes - 1, 1.0, 0.0) * jnp.where(column < lanes, 1.0, 0.0)
    return (before + after).astype(jnp.bfloat16)


def gather(field, around, before, matrix, row, count):
    here = field[pl.ds(row, count)]
    lanes = here.shape[-1]
    flat = here.reshape(-1, lanes)
    high = flat.astype(jnp.bfloat16)
    low = (flat - high.astype(jnp.float32)).astype(jnp.bfloat16)
    found = jnp.dot(
        jnp.concatenate([high, low], axis=1), matrix[...], preferred_element_type=jnp.float32
    )
    around[pl.ds(row, count)] = found[:, :lanes].reshape(here.shape)
    before[pl.ds(row, count)] = found[:, lanes:].reshape(here.shape)


def take_steps(field, mobile, mobile_before, matrix, z_around, z_before, length):
    matrix[...] = z_neighbours(field.shape[-1])

    def at(row):
        here, before = field[row], z_before[row]
        square = here * here
        around = (field[row - 1] + field[row + 1]) + (y_shifted(here, 1) + y_shifted(here, -1))
        potential = here * (square + 5.0) - (around + z_around[row])
        motion = mobile[row] / (1.0 + square)
        return potential, motion, mobile_before[row] / (1.0 + before * before)

    def one_row(row, carried):
        potential, motion, motion_before, inflow = carried
        ahead = at(row + 1)
        outflow = (motion + ahead[1]) * (ahead[0] - potential)
        change = outflow - inflow
        flow = (motion + y_shifted(motion, 1)) * (potential - y_shifted(potential, 1))
        change = change + (y_shifted(flow, -1) - flow)
        flow = (motion + motion_before) * (potential - z_shifted(potential, 1))
        change = change + (z_shifted(flow, -1) - flow)
        field[row] = field[row] + change
        return (*ahead, outflow)

    for step in range(STEPS):
        first, last = 2 * step + 2, length - 2 * step - 2
        for row in range(first - 1, last + 1, CHUNK):
            gather(field, z_around, z_before, matrix, row, min(CHUNK, last + 1 - row))
        before, now = at(first - 1), at(first)
        inflow = (before[1] + now[1]) * (now[0] - before[0])
        lax.fori_loop(first, last, one_row, (*now, inflow), unroll=UNROLL)


def pack_kernel(field, mobility, out, held, semaphores):
    copies = [
        pltpu.make_async_copy(source, held.at[i], semaphores.at[i])
        for i, source in enumerate((field, mobility))
    ]
    for copy in copies:
        copy.start()
    for i, copy in enumerate(copies):
        copy.wait()
        for row in range(field.shape[0]):
            fold(held.at[i, row], out, (i, row), 0.5 * time_step if i else None)


def shift_kernel(mobile, mobile_before):
    def shift_row(row, carried):
        mobile_before[row] = z_shifted(mobile[row], 1)
        return carried

    lax.fori_loop(0, mobile.shape[0], shift_row, 0, unroll=UNROLL)


def first_kernel(index_ref, *refs):
    pieces, out, mobile, window, mobile_before, *scratch = refs[:9], *refs[9:]
    rows = out.shape[0]
    fill(window, index_ref[0], [piece.at[0] for piece in pieces], rows)
    fill(mobile, index_ref[0], [piece.at[1] for piece in pieces], rows)
    shift_kernel(mobile, mobile_before)
    take_steps(window, mobile, mobile_before, *scratch, 9 * rows)
    out[...] = window[pl.ds(4 * rows, rows)]


def later_kernel(index_ref, *refs):
    pieces, mobile, mobile_before, out, window, *scratch = refs[:9], *refs[9:]
    rows = out.shape[0]
    fill(window, index_ref[0], pieces, rows)
    take_steps(window, mobile, mobile_before, *scratch, 9 * rows)
    out[...] = window[pl.ds(4 * rows, rows)]


def squares_of(own, after):
    return jnp.sum(jnp.square(after[...] - own[...]), axis=(0, 1, 2))[None]


def mixing(cycle, image, lower_ref, weight_ref):
    from_left = lower_ref[0, cycle] < image
    weight = weight_ref[0, cycle]
    rest = 1.0 - weight
    return from_left, jnp.where(from_left, weight, rest), jnp.where(from_left, rest, weight)


def mix_kernel(cycle, index_ref, lower_ref, weight_ref, own, inside, across, out, total):
    image = index_ref[0]
    even = lax.rem(image, 2) == 0
    from_left, of_other, of_own = mixing(cycle, image, lower_ref, weight_ref)

    def when(condition, do, *refs):
        pl.when(condition)(lambda: do(*refs))

    def measure(after):
        total[...] = squares_of(own, after)

    def write(other):
        for row in range(own.shape[0]):
            out[row] = of_other * other[row] + of_own * own[row]

    when(even, measure, inside)
    when(jnp.logical_not(even), measure, across)
    when(from_left != even, write, inside)
    when(from_left == even, write, across)


def halves(rows):
    lanes = rows[0].shape[-1]
    lane = lax.broadcasted_iota(jnp.int32, rows[0].shape, 1)
    first, second = (row + pltpu.roll(row, lanes // 2, 1) for row in rows)
    return jnp.where(lane < lanes // 2, first, second)


def gap_kernel(own, right, earlier, everyone):
    row = halves((earlier[...], squares_of(own, right)))
    everyone[...] = jnp.broadcast_to(row[None], everyone.shape)


def final_mix_kernel(index_ref, lower_ref, weight_ref, own, left, right, out):
    from_left, of_other, of_own = mixing(CYCLES - 1, index_ref[0], lower_ref, weight_ref)

    def write(other):
        for row in range(own.shape[0]):
            unfold(of_other * other[row] + of_own * own[row], out.at[row])

    @pl.when(from_left)
    def _():
        write(left)

    @pl.when(jnp.logical_not(from_left))
    def _():
        write(right)


def length_kernel(cells, images, index_ref, gaps, length):
    lanes = gaps.shape[-1]
    each = jnp.sum(gaps[...].reshape(images, -1, lanes), axis=1)
    early = lax.broadcasted_iota(jnp.int32, each.shape, 1) < lanes // 2
    position = lax.broadcasted_iota(jnp.int32, each.shape, 0)
    lane = lax.broadcasted_iota(jnp.int32, length.shape, 1)
    result = jnp.zeros(length.shape, jnp.float32)
    for cycle, chosen in enumerate((early, jnp.logical_not(early))):
        total = jnp.sum(jnp.where(chosen, each, 0.0), axis=1, keepdims=True)
        distance = jnp.sqrt(total / cells + epsilon)
        reached = jnp.sum(jnp.where(position[:, :1] < index_ref[0], distance, 0.0), axis=0, keepdims=True)
        result = jnp.where(lane == cycle, reached, result)
    length[...] = result


def shaped(*shape):
    return jax.ShapeDtypeStruct(shape, jnp.float32)


def cycles(field, mobility, lower, weights):
    rows, depth, lanes = field.shape[1:]
    slab = (rows, depth // SUBLANES, SUBLANES, lanes)
    wide = (9 * rows,) + slab[1:]
    window = [pltpu.VMEM(wide, jnp.float32)]
    scratch = [pltpu.VMEM((2 * lanes, 2 * lanes), jnp.bfloat16), *window, *window]
    image_count, domain_count = lax.axis_size("image"), lax.axis_size("domain")
    image_index = lax.axis_index("image")[None]
    index = lax.axis_index("domain")
    lower, weights = lower.T, weights.T
    cells = rows * domain_count * depth * lanes

    packed = pl.pallas_call(
        pack_kernel,
        out_shape=shaped(2, *slab),
        in_specs=[HBM] * 2,
        out_specs=VMEM,
        scratch_shapes=[
            pltpu.VMEM((2, rows, depth, lanes), jnp.float32),
            pltpu.SemaphoreType.DMA((2,)),
        ],
        compiler_params=PARAMS,
    )(field[0], mobility)
    phase, mobile = pl.pallas_call(
        first_kernel,
        out_shape=(shaped(*slab), shaped(*wide)),
        in_specs=[SMEM] + [VMEM] * 9,
        out_specs=(VMEM, VMEM),
        scratch_shapes=[*window, *window, *scratch],
        compiler_params=PARAMS,
    )(index[None], *halo_pieces(packed, index))
    mobile_before = pl.pallas_call(
        shift_kernel,
        out_shape=shaped(*wide),
        in_specs=[VMEM],
        out_specs=VMEM,
        compiler_params=PARAMS,
    )(mobile)

    totals = []
    for cycle in range(CYCLES - 1):
        across = exchanged(phase, "image", lambda i, size: i - side(i, 1))
        inside = exchanged(phase, "image", partner_inside(1))
        phase, total = pl.pallas_call(
            lambda *refs, cycle=cycle: mix_kernel(cycle, *refs),
            out_shape=(shaped(*slab), shaped(1, lanes)),
            in_specs=[SMEM] * 3 + [VMEM] * 3,
            out_specs=(VMEM, VMEM),
            compiler_params=PARAMS,
        )(image_index, lower, weights, phase, inside, across)
        totals.append(total)
        phase = pl.pallas_call(
            later_kernel,
            out_shape=shaped(*slab),
            in_specs=[SMEM] + [VMEM] * 11,
            out_specs=VMEM,
            scratch_shapes=[*window, *scratch],
            compiler_params=PARAMS,
        )(index[None], *halo_pieces(phase, index), mobile, mobile_before)
    right = passed_along(phase, -1)
    left = passed_along(phase, 1)
    everyone = pl.pallas_call(
        gap_kernel,
        out_shape=shaped(image_count * domain_count, 1, lanes),
        in_specs=[VMEM] * 3,
        out_specs=VMEM,
        compiler_params=PARAMS,
    )(phase, right, *totals)
    gaps = lax.all_to_all(everyone, ("image", "domain"), 0, 0)
    evolved = pl.pallas_call(
        final_mix_kernel,
        out_shape=shaped(rows, depth, lanes),
        in_specs=[SMEM] * 3 + [VMEM] * 3,
        out_specs=VMEM,
        compiler_params=PARAMS,
    )(image_index, lower, weights, phase, left, right)
    arclength = pl.pallas_call(
        lambda *refs: length_kernel(cells, image_count, *refs),
        out_shape=shaped(1, CYCLES),
        in_specs=[SMEM, VMEM],
        out_specs=VMEM,
        compiler_params=PARAMS,
    )(image_index, gaps)
    return evolved[None], arclength.T


def solution(mesh):
    return jax.shard_map(
        cycles,
        mesh=mesh,
        in_specs=(
            P("image", "domain", None, None),
            P("domain", None, None),
            P(None, "image"),
            P(None, "image"),
        ),
        out_specs=(P("image", "domain", None, None), P(None, "image")),
        check_vma=False,
    )
```

```python
import jax
import jax.numpy as jnp
from jax import lax
from jax.experimental import pallas as pl
from jax.experimental.pallas import tpu as pltpu
from jax.sharding import PartitionSpec as P

STEPS = 8
CYCLES = 2
SUBLANES = 8
UNROLL = 10
CHUNK = 8

time_step = 0.008
epsilon = 1e-06

VMEM = pl.BlockSpec(memory_space=pltpu.VMEM)
SMEM = pl.BlockSpec(memory_space=pltpu.SMEM)
HBM = pl.BlockSpec(memory_space=pltpu.HBM)
PARAMS = pltpu.CompilerParams(vmem_limit_bytes=16 << 20)


def exchanged(value, axis, partner):
    size = lax.axis_size(axis)
    pairs = [(i, partner(i, size)) for i in range(size)]
    return lax.ppermute(value, axis, [(i, j) for i, j in pairs if 0 <= j < size])


def passed_along(value, steps):
    count = lax.axis_size("image")
    first, last = (max(0, -steps), min(count, count - steps))
    return lax.ppermute(value, "image", [(i, i + steps) for i in range(first, last)])


def side(index, stride):
    return 1 - 2 * (index // stride % 2)


def partner_inside(stride):
    return lambda i, size: i + side(i, stride) * stride


def partner_across(stride):
    return lambda i, size: (i - side(i, stride) * stride) % size


CORE_STARTS = ("core_inside_two", "core_across_two")


def halo_pieces(own):
    straight = []
    for partner, stride in zip((partner_across, partner_inside) * 2, (2, 2, 4, 4)):
        straight.append(exchanged(own, "domain", partner(stride)))
    across_two, inside_two = straight[:2]
    beside = exchanged(own, "domain", partner_inside(1))
    others = {}
    for name, piece in zip(CORE_STARTS, (inside_two, across_two)):
        others[name] = exchanged(piece, "domain", partner_inside(1))
    last = exchanged(own, "domain", lambda i, size: (i - 3 * side(i, 1)) % size)
    return [own, *straight, beside, others[CORE_STARTS[1]], others[CORE_STARTS[0]], last]


def slab_offsets(index):
    core, two, four = (side(index, stride) for stride in (1, 2, 4))
    straight = (0, -2 * two, 2 * two, -4 * four, 4 * four)
    return straight + (core, core - 2 * two, core + 2 * two, -3 * core)


def fill(window, index, pieces, rows):
    for offset, piece in zip(slab_offsets(index), pieces):
        start = pl.multiple_of((4 + offset) * rows, rows)
        window[pl.ds(start, rows)] = piece[...]


def fold(plane, target, place, scale=None):
    folds = target.shape[-3]
    for v in range(folds):
        part = plane[pl.ds(v, SUBLANES, stride=folds), :]
        target[(*place, v)] = part if scale is None else part * scale


def unfold(value, target):
    for v in range(value.shape[0]):
        target[pl.ds(v, SUBLANES, stride=value.shape[0]), :] = value[v]


def y_shifted(value, offset):
    if offset == 1:
        return jnp.concatenate([pltpu.roll(value[-1:], 1, 1), value[:-1]], axis=0)
    return jnp.concatenate([value[1:], pltpu.roll(value[:1], SUBLANES - 1, 1)], axis=0)


def z_shifted(value, offset):
    return pltpu.roll(value, offset % value.shape[2], 2)


def z_neighbours(lanes):
    shape = (2 * lanes, 2 * lanes)
    source = lax.rem(lax.broadcasted_iota(jnp.int32, shape, 0), lanes)
    column = lax.broadcasted_iota(jnp.int32, shape, 1)
    ahead = lax.rem(lax.rem(column, lanes) - source + lanes, lanes)
    before = jnp.where(ahead == 1, 1.0, 0.0)
    after = jnp.where(ahead == lanes - 1, 1.0, 0.0) * jnp.where(column < lanes, 1.0, 0.0)
    return (before + after).astype(jnp.bfloat16)


def gather(field, around, before, matrix, row, count):
    here = field[pl.ds(row, count)]
    lanes = here.shape[-1]
    flat = here.reshape(-1, lanes)
    high = flat.astype(jnp.bfloat16)
    low = (flat - high.astype(jnp.float32)).astype(jnp.bfloat16)
    found = jnp.dot(
        jnp.concatenate([high, low], axis=1), matrix[...], preferred_element_type=jnp.float32
    )
    around[pl.ds(row, count)] = found[:, :lanes].reshape(here.shape)
    before[pl.ds(row, count)] = found[:, lanes:].reshape(here.shape)


def unrolled(count):
    return max(n for n in range(1, UNROLL + 1) if count % n == 0)


def take_steps(field, mobile, mobile_before, matrix, z_around, z_before, length):
    matrix[...] = z_neighbours(field.shape[-1])

    def at(row):
        here, before = field[row], z_before[row]
        square = here * here
        around = (field[row - 1] + field[row + 1]) + (y_shifted(here, 1) + y_shifted(here, -1))
        potential = here * (square + 5.0) - (around + z_around[row])
        motion = mobile[row] / (1.0 + square)
        return potential, motion, mobile_before[row] / (1.0 + before * before)

    def one_row(row, carried):
        potential, motion, motion_before, inflow = carried
        ahead = at(row + 1)
        outflow = (motion + ahead[1]) * (ahead[0] - potential)
        change = outflow - inflow
        flow = (motion + y_shifted(motion, 1)) * (potential - y_shifted(potential, 1))
        change = change + (y_shifted(flow, -1) - flow)
        flow = (motion + motion_before) * (potential - z_shifted(potential, 1))
        change = change + (z_shifted(flow, -1) - flow)
        field[row] = field[row] + change
        return (*ahead, outflow)

    for step in range(STEPS):
        first, last = 2 * step + 2, length - 2 * step - 2
        for row in range(first - 1, last + 1, CHUNK):
            gather(field, z_around, z_before, matrix, row, min(CHUNK, last + 1 - row))
        before, now = at(first - 1), at(first)
        inflow = (before[1] + now[1]) * (now[0] - before[0])
        lax.fori_loop(first, last, one_row, (*now, inflow), unroll=unrolled(last - first))


def pack_kernel(field, mobility, out, held, semaphores):
    copies = [
        pltpu.make_async_copy(source, held.at[i], semaphores.at[i])
        for i, source in enumerate((field, mobility))
    ]
    for copy in copies:
        copy.start()
    for i, copy in enumerate(copies):
        copy.wait()
        for row in range(field.shape[0]):
            fold(held.at[i, row], out, (i, row), 0.5 * time_step if i else None)


def shift_kernel(mobile, mobile_before):
    def shift_row(row, carried):
        mobile_before[row] = z_shifted(mobile[row], 1)
        return carried

    lax.fori_loop(0, mobile.shape[0], shift_row, 0, unroll=unrolled(mobile.shape[0]))


def first_kernel(index_ref, *refs):
    pieces, out, mobile, window, mobile_before, *scratch = refs[:9], *refs[9:]
    rows = out.shape[0]
    fill(window, index_ref[0], [piece.at[0] for piece in pieces], rows)
    fill(mobile, index_ref[0], [piece.at[1] for piece in pieces], rows)
    shift_kernel(mobile, mobile_before)
    take_steps(window, mobile, mobile_before, *scratch, 9 * rows)
    out[...] = window[pl.ds(4 * rows, rows)]


def later_kernel(index_ref, *refs):
    pieces, mobile, mobile_before, out, window, *scratch = refs[:9], *refs[9:]
    rows = out.shape[0]
    fill(window, index_ref[0], pieces, rows)
    take_steps(window, mobile, mobile_before, *scratch, 9 * rows)
    out[...] = window[pl.ds(4 * rows, rows)]


def squares_of(own, after):
    return jnp.sum(jnp.square(after[...] - own[...]), axis=(0, 1, 2))[None]


def mixing(cycle, image, lower_ref, weight_ref):
    from_left = lower_ref[0, cycle] < image
    weight = weight_ref[0, cycle]
    rest = 1.0 - weight
    return from_left, jnp.where(from_left, weight, rest), jnp.where(from_left, rest, weight)


def mix_kernel(cycle, index_ref, lower_ref, weight_ref, own, inside, across, out, total):
    image = index_ref[0]
    even = lax.rem(image, 2) == 0
    from_left, of_other, of_own = mixing(cycle, image, lower_ref, weight_ref)

    def when(condition, do, *refs):
        pl.when(condition)(lambda: do(*refs))

    def measure(after):
        total[...] = squares_of(own, after)

    def write(other):
        for row in range(own.shape[0]):
            out[row] = of_other * other[row] + of_own * own[row]

    when(even, measure, inside)
    when(jnp.logical_not(even), measure, across)
    when(from_left != even, write, inside)
    when(from_left == even, write, across)


def halves(rows):
    lanes = rows[0].shape[-1]
    lane = lax.broadcasted_iota(jnp.int32, rows[0].shape, 1)
    first, second = (row + pltpu.roll(row, lanes // 2, 1) for row in rows)
    return jnp.where(lane < lanes // 2, first, second)


def gap_kernel(own, right, earlier, everyone):
    row = halves((earlier[...], squares_of(own, right)))
    everyone[...] = jnp.broadcast_to(row[None], everyone.shape)


def final_mix_kernel(index_ref, lower_ref, weight_ref, own, left, right, out):
    from_left, of_other, of_own = mixing(CYCLES - 1, index_ref[0], lower_ref, weight_ref)

    def write(other):
        for row in range(own.shape[0]):
            unfold(of_other * other[row] + of_own * own[row], out.at[row])

    @pl.when(from_left)
    def _():
        write(left)

    @pl.when(jnp.logical_not(from_left))
    def _():
        write(right)


def length_kernel(cells, images, index_ref, gaps, length):
    lanes = gaps.shape[-1]
    each = jnp.sum(gaps[...].reshape(images, -1, lanes), axis=1)
    early = lax.broadcasted_iota(jnp.int32, each.shape, 1) < lanes // 2
    position = lax.broadcasted_iota(jnp.int32, each.shape, 0)
    lane = lax.broadcasted_iota(jnp.int32, length.shape, 1)
    result = jnp.zeros(length.shape, jnp.float32)
    for cycle, chosen in enumerate((early, jnp.logical_not(early))):
        total = jnp.sum(jnp.where(chosen, each, 0.0), axis=1, keepdims=True)
        distance = jnp.sqrt(total / cells + epsilon)
        reached = jnp.sum(jnp.where(position[:, :1] < index_ref[0], distance, 0.0), axis=0, keepdims=True)
        result = jnp.where(lane == cycle, reached, result)
    length[...] = result


def shaped(*shape):
    return jax.ShapeDtypeStruct(shape, jnp.float32)


def cycles(field, mobility, lower, weights):
    rows, depth, lanes = field.shape[1:]
    slab = (rows, depth // SUBLANES, SUBLANES, lanes)
    wide = (9 * rows,) + slab[1:]
    window = [pltpu.VMEM(wide, jnp.float32)]
    scratch = [pltpu.VMEM((2 * lanes, 2 * lanes), jnp.bfloat16), *window, *window]
    image_count, domain_count = lax.axis_size("image"), lax.axis_size("domain")
    image_index = lax.axis_index("image")[None]
    index = lax.axis_index("domain")
    lower, weights = lower.T, weights.T
    cells = rows * domain_count * depth * lanes

    packed = pl.pallas_call(
        pack_kernel,
        out_shape=shaped(2, *slab),
        in_specs=[HBM] * 2,
        out_specs=VMEM,
        scratch_shapes=[
            pltpu.VMEM((2, rows, depth, lanes), jnp.float32),
            pltpu.SemaphoreType.DMA((2,)),
        ],
        compiler_params=PARAMS,
    )(field[0], mobility)
    phase, mobile = pl.pallas_call(
        first_kernel,
        out_shape=(shaped(*slab), shaped(*wide)),
        in_specs=[SMEM] + [VMEM] * 9,
        out_specs=(VMEM, VMEM),
        scratch_shapes=[*window, *window, *scratch],
        compiler_params=PARAMS,
    )(index[None], *halo_pieces(packed))
    mobile_before = pl.pallas_call(
        shift_kernel,
        out_shape=shaped(*wide),
        in_specs=[VMEM],
        out_specs=VMEM,
        compiler_params=PARAMS,
    )(mobile)

    totals = []
    for cycle in range(CYCLES - 1):
        across = exchanged(phase, "image", lambda i, size: i - side(i, 1))
        inside = exchanged(phase, "image", partner_inside(1))
        phase, total = pl.pallas_call(
            lambda *refs, cycle=cycle: mix_kernel(cycle, *refs),
            out_shape=(shaped(*slab), shaped(1, lanes)),
            in_specs=[SMEM] * 3 + [VMEM] * 3,
            out_specs=(VMEM, VMEM),
            compiler_params=PARAMS,
        )(image_index, lower, weights, phase, inside, across)
        totals.append(total)
        phase = pl.pallas_call(
            later_kernel,
            out_shape=shaped(*slab),
            in_specs=[SMEM] + [VMEM] * 11,
            out_specs=VMEM,
            scratch_shapes=[*window, *scratch],
            compiler_params=PARAMS,
        )(index[None], *halo_pieces(phase), mobile, mobile_before)
    right = passed_along(phase, -1)
    left = passed_along(phase, 1)
    everyone = pl.pallas_call(
        gap_kernel,
        out_shape=shaped(image_count * domain_count, 1, lanes),
        in_specs=[VMEM] * 3,
        out_specs=VMEM,
        compiler_params=PARAMS,
    )(phase, right, *totals)
    gaps = lax.all_to_all(everyone, ("image", "domain"), 0, 0)
    evolved = pl.pallas_call(
        final_mix_kernel,
        out_shape=shaped(rows, depth, lanes),
        in_specs=[SMEM] * 3 + [VMEM] * 3,
        out_specs=VMEM,
        compiler_params=PARAMS,
    )(image_index, lower, weights, phase, left, right)
    arclength = pl.pallas_call(
        lambda *refs: length_kernel(cells, image_count, *refs),
        out_shape=shaped(1, CYCLES),
        in_specs=[SMEM, VMEM],
        out_specs=VMEM,
        compiler_params=PARAMS,
    )(image_index, gaps)
    return evolved[None], arclength.T


def solution(mesh):
    return jax.shard_map(
        cycles,
        mesh=mesh,
        in_specs=(
            P("image", "domain", None, None),
            P("domain", None, None),
            P(None, "image"),
            P(None, "image"),
        ),
        out_specs=(P("image", "domain", None, None), P(None, "image")),
        check_vma=False,
    )
```
